32 devices in a mesh: sample: 4 (over x, core), space: 8 (over z, y).
Axes of the slice: x: 2, y: 2, z: 4, core: 2. Of those that a mesh axis runs over, the one named last changes fastest.
Arguments:
- activations: bfloat16 [4, 64, 32, 1024], P('sample', 'space'), may hold values from -6 to 6
- open_cells: int32 [4, 64, 512], P('sample', 'space'), may hold values 0 or 1
- wind_class: int32 [4], P('sample'), may hold values from 0 to 7
- w_early: bfloat16 [3, 3, 3, 64, 128], replicated, may hold values from -0.15625 to 0.15625
- bias_table: float32 [8, 128], replicated, may hold values from -3 to 3
- w_deep: bfloat16 [2, 2, 2, 128, 256], replicated, may hold values from -0.1875 to 0.1875
- cotangent: bfloat16 [4, 16, 8, 1024], P('sample', 'space'), may hold values from -0.119628906 to 0.119628906
Outputs:
- deep: bfloat16 [4, 16, 8, 1024], P('sample', 'space')
- grad_deep: float32 [2, 2, 2, 128, 256], replicated
- grad_early: float32 [3, 3, 3, 64, 128], replicated
The draws below stay inside these ranges and needn't reach their ends.
All inputs are finite; a program needn't handle non-finite values. No bound on the sum of `open_cells` on one device may be relied on, other than what follows from the above.
Results may differ from the reference program's by a relative error of at most 0.005.
Values may be sent and summed in bfloat16 or wider, within the bound.
No kernel may reach another device: no remote copies, remote signals or barrier semaphores. Data moves between devices by JAX's collectives and lax.ppermute only.
A program may use at most 64 MiB of HBM per device.

```python
import jax
import jax.numpy as jnp
from jax import lax

C0 = 64
C1 = 128
C2 = 256
CLASSES = 8
NY = 32
NX = 16
SAMPLES = 4
NZ = 64


def set_ends(values, stream_key, low, high):
    longest = values.shape.index(max(values.shape))
    spots = []
    for shift in (0, 1):
        where = [jax.random.randint(jax.random.fold_in(stream_key, axis), (), 0, length) for axis, length in enumerate(values.shape)]
        where[longest] = (where[longest] + shift) % values.shape[longest]
        spots.append(tuple(where))
    return values.at[spots[0]].set(low).at[spots[1]].set(high)


def block_scale(own_key, shape, cuts, smallest, high):
    factor_of, own = 1.0, jax.random.fold_in(own_key, 6)
    for dim, shards_of in cuts:
        steps = jnp.exp(jax.random.uniform(jax.random.fold_in(own, dim), (shards_of,), jnp.float32, smallest / len(cuts), high / len(cuts)))
        factor_of = factor_of * jnp.repeat(steps, shape[dim] // shards_of).reshape([-1 if axis == dim else 1 for axis in range(len(shape))])
    return factor_of


def centred(key, shape, width, bound, split=(), held_as=jnp.bfloat16):
    array = jax.random.normal(key, shape, jnp.float32) * width
    if len(split) > 0:
        array = block_scale(key, shape, split, -0.22, 0.18) * array
    return jnp.clip(array, min=-bound, max=bound).astype(held_as)


def setup_inputs(seed: int = 0) -> dict:
    arg_keys = jax.random.split(jax.random.key(seed), 8)
    return {
        "activations": centred(arg_keys[0], (SAMPLES, NZ, NY, NX * C0), 1.0, 6.0, ((0, 4), (1, 8))),
        "open_cells": set_ends((jax.random.randint(arg_keys[1], (SAMPLES, NZ, NY * NX), 0, 4) < 3).astype(jnp.int32), jax.random.fold_in(arg_keys[1], 1), 0, 1),
        "wind_class": set_ends(jax.random.randint(arg_keys[2], (SAMPLES,), 0, CLASSES), jax.random.fold_in(arg_keys[2], 1), 0, CLASSES - 1).astype(jnp.int32),
        "w_early": centred(arg_keys[3], (3, 3, 3, C0, C1), (27 * C0) ** -0.5, 0.15625),
        "bias_table": centred(arg_keys[4], (CLASSES, C1), 0.5, 3.0, (), jnp.float32),
        "w_deep": centred(arg_keys[5], (2, 2, 2, C1, C2), (8 * C1) ** -0.5, 0.1875),
        "cotangent": centred(arg_keys[6], (SAMPLES, NZ // 4, NY // 4, (NX // 4) * C2), 0.02, 0.119628906, ((0, 4), (1, 8))),
    }


SLOPE = 0.3

def early_forward(padded, w_early, bias):
    out = lax.conv_general_dilated(padded[None], w_early, (2, 2, 2), ((0, 0), (0, 0), (0, 0)), dimension_numbers=('NDHWC', 'DHWIO', 'NDHWC'), preferred_element_type=jnp.float32)
    return out[0] + bias

def deep_terms(hidden, w_deep, upstream):
    zh, yh, xh, c1 = hidden.shape
    c2 = w_deep.shape[4]
    patches = hidden.reshape(zh // 2, 2, yh // 2, 2, xh // 2, 2, c1).transpose(0, 2, 4, 1, 3, 5, 6).reshape(-1, 8 * c1)
    out = jnp.dot(patches, w_deep.reshape(8 * c1, c2), preferred_element_type=jnp.float32)
    flat_up = upstream.reshape(-1, c2)
    grad_w = lax.dot_general(patches, flat_up, (((0,), (0,)), ((), ())), preferred_element_type=jnp.float32).reshape(2, 2, 2, c1, c2)
    back = lax.dot_general(flat_up, w_deep.reshape(8, c1, c2), (((1,), (2,)), ((), ())), preferred_element_type=jnp.float32)
    back = back.reshape(zh // 2, yh // 2, xh // 2, 2, 2, 2, c1).transpose(0, 3, 1, 4, 2, 5, 6).reshape(zh, yh, xh, c1)
    return (out, grad_w, back)

def early_grad(padded, delta):
    zo, yo, xo, c1 = delta.shape
    c0 = padded.shape[3]
    flat_delta = delta.reshape(-1, c1)
    pieces = []
    for a in range(3):
        for b in range(3):
            for c in range(3):
                piece = lax.slice(padded, (a, b, c, 0), (a + 2 * zo - 1, b + 2 * yo - 1, c + 2 * xo - 1, c0), (2, 2, 2, 1)).reshape(-1, c0)
                pieces.append(lax.dot_general(piece, flat_delta, (((0,), (0,)), ((), ())), preferred_element_type=jnp.float32))
    return jnp.stack(pieces).reshape(3, 3, 3, c0, c1)

def reference(activations, open_cells, wind_class, w_early, bias_table, w_deep, cotangent):

    def one_sample(items):
        acts, opens, kind, upstream = items
        field = acts.reshape(NZ, NY, NX, C0) * opens.reshape(NZ, NY, NX, 1).astype(jnp.bfloat16)
        chosen = jnp.arange(CLASSES, dtype=jnp.int32)[:, None] == kind
        bias = lax.optimization_barrier(jnp.sum(jnp.where(chosen, bias_table, jnp.zeros_like(bias_table)), axis=0))
        padded = jnp.pad(field, ((1, 0), (1, 0), (1, 0), (0, 0)))
        pre = early_forward(padded, w_early, bias)
        hidden = jnp.where(pre > 0, pre, SLOPE * pre).astype(jnp.bfloat16)
        upstream = upstream.reshape(NZ // 4, NY // 4, NX // 4, C2)
        out, grad_w, back = deep_terms(hidden, w_deep, upstream)
        delta = (back * jnp.where(pre > 0, 1.0, SLOPE)).astype(jnp.bfloat16)
        grad_e = early_grad(padded, delta)
        return (out.astype(jnp.bfloat16).reshape(NZ // 4, NY // 4, NX // 4 * C2), grad_w, grad_e)
    deep, grads_deep, grads_early = lax.map(one_sample, (activations, open_cells, wind_class, cotangent))
    return (deep, lax.optimization_barrier(jnp.sum(grads_deep, axis=0)), lax.optimization_barrier(jnp.sum(grads_early, axis=0)))
```

```python
import jax
import jax.numpy as jnp
from jax import lax
from jax.experimental import pallas as pl
from jax.experimental.pallas import tpu as pltpu
from jax.sharding import PartitionSpec as P

SLOPE = 0.3
BF16 = jnp.bfloat16
F32 = jnp.float32

DEPTH, ROWS, CELLS, C0, C1, C2 = 8, 32, 16, 64, 128, 256
PAIR = 2 * C0
WIDE = CELLS * C0
CHUNKS = 8
DEEP_ROWS = 8 * C1 * C2 // 128 // CHUNKS
EARLY_ROWS = 27 * C0 // CHUNKS
CHUNK_ROWS = DEEP_ROWS + EARLY_ROWS
VMEM_BYTES = 48 * 1024 * 1024


def iota(shape, dim):
    return lax.broadcasted_iota(jnp.int32, shape, dim)


def masked_rows(acts, opens):
    planes = opens.shape[0]
    cells = ROWS * CELLS
    own = (iota((ROWS, cells), 1) // CELLS) == iota((ROWS, cells), 0)
    spread = jnp.concatenate(
        [jnp.where(own, opens[z : z + 1, :], 0).astype(F32).astype(BF16) for z in range(planes)], axis=0
    )
    pick = ((iota((cells, 128), 0) % CELLS) == iota((cells, 128), 1)).astype(F32).astype(BF16)
    by_cell = jnp.dot(spread, pick, preferred_element_type=F32).astype(BF16)
    widen = (iota((128, WIDE), 0) == (iota((128, WIDE), 1) // C0)).astype(F32).astype(BF16)
    mask = jnp.dot(by_cell, widen, preferred_element_type=F32).astype(BF16)
    return acts * mask


def edge_kernel(acts_ref, opens_ref, edge_ref):
    edge_ref[...] = masked_rows(acts_ref[0], opens_ref[DEPTH - 1 : DEPTH, :])


def row_of_slot(q):
    return 2 * (q % 8) + q // 8


def local_kernel(
    kind_ref, acts_ref, opens_ref, below_ref, w1_ref, bias_ref, w2_ref, cot_ref,
    deep_ref, keep_ref, send_ref,
    even_ref, odd_ref, patch_ref, early_ref,
):
    core = lax.axis_index("sample") % 2
    place = ((lax.axis_index("sample") // 2) % 2) * 2 + lax.axis_index("space") % 2

    field = masked_rows(acts_ref[...].reshape(DEPTH * ROWS, WIDE), opens_ref[...])
    half = 3 * 64
    r = iota((2 * half, DEPTH * ROWS), 0)
    par = (r >= half).astype(jnp.int32)
    s = r - half * par
    y = 2 * row_of_slot(s % 16) + s // 64 - 1
    z = 2 * ((s % 64) // 16) + par
    want = jnp.where(y >= 0, z * ROWS + y, -1)
    pick = (iota(r.shape, 1) == want).astype(F32).astype(BF16)
    rows = jnp.dot(pick, field, preferred_element_type=F32).astype(BF16)
    r = iota((48, ROWS), 0)
    y = 2 * row_of_slot(r % 16) + r // 16 - 1
    pick = (iota(r.shape, 1) == y).astype(F32).astype(BF16)
    rows_below = jnp.dot(pick, below_ref[...], preferred_element_type=F32).astype(BF16)
    for b in range(3):
        even_ref[b, :, :PAIR] = jnp.zeros((64, PAIR), BF16)
        odd_ref[b, :, :PAIR] = jnp.zeros((80, PAIR), BF16)
        even_ref[b, :, PAIR:] = rows[b * 64 : (b + 1) * 64]
        odd_ref[b, :16, PAIR:] = rows_below[b * 16 : (b + 1) * 16]
        odd_ref[b, 16:, PAIR:] = rows[half + b * 64 : half + (b + 1) * 64]

    def windows(a, b):
        ref, top = (even_ref, 0) if a == 1 else (odd_ref, 8 * a)
        return jnp.concatenate(
            [ref[b, top : top + 64, x * PAIR : (x + 2) * PAIR] for x in range(CELLS // 2)], axis=0
        )

    classes = bias_ref.shape[0]
    chosen = iota((classes, C1), 0) == kind_ref[0]
    bias = jnp.sum(jnp.where(chosen, bias_ref[...], 0.0), axis=0, keepdims=True)
    pre = jnp.zeros((512, C1), F32)
    for a in range(3):
        for b in range(3):
            w = jnp.concatenate([jnp.zeros((C0, C1), BF16), w1_ref[a * 3 + b]], axis=0)
            pre = pre + jnp.dot(windows(a, b), w, preferred_element_type=F32)
    pre = pre + bias
    hidden = jnp.where(pre > 0, pre, SLOPE * pre)

    def piece(xs, zs, a, b, c):
        return (2 * xs + c) * 64 + (2 * zs + a) * 16 + b * 8

    pieces = [(xs, zs) for xs in range(CELLS // 4) for zs in range(DEPTH // 4)]
    taps = [(a, b, c) for a in range(2) for b in range(2) for c in range(2)]
    cot = jnp.concatenate([cot_ref[:, x * C2 : (x + 1) * C2] for x in range(CELLS // 4)], axis=0)
    out = jnp.zeros((64, C2), F32)
    delta_at = {}
    for t, (a, b, c) in enumerate(taps):
        starts = [piece(xs, zs, a, b, c) for xs, zs in pieces]
        patch = jnp.concatenate([hidden[at : at + 8] for at in starts], axis=0).astype(BF16)
        patch_ref[t] = patch
        out = out + jnp.dot(patch, w2_ref[t], preferred_element_type=F32)
        back = lax.dot_general(cot, w2_ref[t], (((1,), (1,)), ((), ())), preferred_element_type=F32)
        for k, at in enumerate(starts):
            delta_at[at] = back[k * 8 : (k + 1) * 8]
    out = out.astype(BF16)
    for x in range(CELLS // 4):
        deep_ref[:, x * C2 : (x + 1) * C2] = out[x * 16 : (x + 1) * 16]
    back = jnp.concatenate([delta_at[at] for at in sorted(delta_at)], axis=0)
    delta = (back * jnp.where(pre > 0, 1.0, SLOPE)).astype(BF16)

    for a in range(3):
        for b in range(3):
            grad = lax.dot_general(
                windows(a, b), delta, (((0,), (0,)), ((), ())), preferred_element_type=F32
            )
            at = (a * 3 + b) * 3 * C0
            early_ref[at : at + 3 * C0] = grad[C0:]

    for far in range(2):
        for m in range(4):
            chunk = ((core + far) % 2) * 4 + (place ^ m)
            grad = lax.dot_general(
                patch_ref[chunk], cot, (((0,), (0,)), ((), ())), preferred_element_type=F32
            )
            early = early_ref[pl.ds(pl.multiple_of(chunk * EARLY_ROWS, 8), EARLY_ROWS), :]
            ref, kind = (send_ref, BF16) if far else (keep_ref, F32)
            ref[m, :C1] = grad[:, :128].astype(kind)
            ref[m, C1 : 2 * C1] = grad[:, 128:].astype(kind)
            ref[m, 2 * C1 :] = early.astype(kind)


def spread_kernel(near_ref, far_ref, deep_ref, early_ref):
    core = lax.axis_index("sample") % 2
    place = ((lax.axis_index("sample") // 2) % 2) * 2 + lax.axis_index("space") % 2
    for far in range(2):
        ref = far_ref if far else near_ref
        for m in range(4):
            chunk = ((core + far) % 2) * 4 + (place ^ m)
            deep_ref[chunk, :, :128] = ref[m, :C1].astype(F32)
            deep_ref[chunk, :, 128:] = ref[m, C1 : 2 * C1].astype(F32)
            at = pl.multiple_of(chunk * EARLY_ROWS, 8)
            early_ref[pl.ds(at, EARLY_ROWS), :] = ref[m, 2 * C1 :].astype(F32)


def swapped(value, sample_bits=0, space_bits=0):
    samples, spaces = lax.axis_size("sample"), lax.axis_size("space")
    pairs = [
        (i * spaces + j, (i ^ sample_bits) * spaces + (j ^ space_bits))
        for i in range(samples)
        for j in range(spaces)
    ]
    return lax.ppermute(value, ("sample", "space"), pairs)


QUAD = ((0, 1), (2, 0), (2, 1))


def total(keep, send):
    near = keep + swapped(send, 1).astype(F32)
    mine = near[0]
    others = near[1:].astype(BF16)
    for k, (i, j) in enumerate(QUAD):
        mine = mine + swapped(others[k], i, j).astype(F32)
    for axis, first in (("space", 2), ("sample", 4)):
        bit = first
        while bit < lax.axis_size(axis):
            own = mine.astype(BF16)
            peer = swapped(own, bit, 0) if axis == "sample" else swapped(own, 0, bit)
            mine = own.astype(F32) + peer.astype(F32)
            bit *= 2
    own = mine.astype(BF16)
    near = jnp.stack([own] + [swapped(own, i, j) for i, j in QUAD])
    return near, swapped(near, 1)


def body(activations, open_cells, wind_class, w_early, bias_table, w_deep, cotangent):
    params = pltpu.CompilerParams(vmem_limit_bytes=VMEM_BYTES)
    acts = activations[0]
    opens = open_cells[0]
    edge = pl.pallas_call(
        edge_kernel,
        grid=(1,),
        in_specs=[
            pl.BlockSpec((1, ROWS, WIDE), lambda i: (DEPTH - 1, 0, 0)),
            pl.BlockSpec((DEPTH, ROWS * CELLS), lambda i: (0, 0)),
        ],
        out_specs=pl.BlockSpec((ROWS, WIDE), lambda i: (0, 0)),
        out_shape=jax.ShapeDtypeStruct((ROWS, WIDE), BF16),
        compiler_params=params,
        name="edge_plane",
    )(acts, opens)
    spaces = lax.axis_size("space")
    below = lax.ppermute(edge, "space", [(i, i + 1) for i in range(spaces - 1)])
    vmem = pl.BlockSpec(memory_space=pltpu.VMEM)
    smem = pl.BlockSpec(memory_space=pltpu.SMEM)
    deep, keep, send = pl.pallas_call(
        local_kernel,
        in_specs=[smem] + [vmem] * 7,
        out_specs=[vmem] * 3,
        out_shape=[
            jax.ShapeDtypeStruct((DEPTH // 4 * ROWS // 4, CELLS // 4 * C2), BF16),
            jax.ShapeDtypeStruct((4, CHUNK_ROWS, 128), F32),
            jax.ShapeDtypeStruct((4, CHUNK_ROWS, 128), BF16),
        ],
        scratch_shapes=[
            pltpu.VMEM((3, 64, WIDE + PAIR), BF16),
            pltpu.VMEM((3, 80, WIDE + PAIR), BF16),
            pltpu.VMEM((8, 64, C1), BF16),
            pltpu.VMEM((27 * C0, C1), F32),
        ],
        compiler_params=params,
        name="local_terms",
    )(
        wind_class,
        acts,
        opens,
        below,
        w_early.reshape(9, 3 * C0, C1),
        bias_table,
        w_deep.reshape(8, C1, C2),
        cotangent.reshape(DEPTH // 4 * ROWS // 4, CELLS // 4 * C2),
    )
    near, far = total(keep, send)
    grad_deep, grad_early = pl.pallas_call(
        spread_kernel,
        in_specs=[vmem] * 2,
        out_specs=[vmem] * 2,
        out_shape=[
            jax.ShapeDtypeStruct((8, C1, C2), F32),
            jax.ShapeDtypeStruct((27 * C0, C1), F32),
        ],
        compiler_params=params,
        name="spread_sums",
    )(near, far)
    return (
        deep.reshape(1, DEPTH // 4, ROWS // 4, CELLS // 4 * C2),
        grad_deep.reshape(w_deep.shape),
        grad_early.reshape(w_early.shape),
    )


def solution(mesh):
    in_specs = (
        P("sample", "space", None, None),
        P("sample", "space", None),
        P("sample"),
        P(),
        P(),
        P(),
        P("sample", "space", None, None),
    )
    out_specs = (P("sample", "space", None, None), P(), P())
    return jax.shard_map(body, mesh=mesh, in_specs=in_specs, out_specs=out_specs, check_vma=False)
```

```python
import jax
import jax.numpy as jnp
from jax import lax
from jax.experimental import pallas as pl
from jax.experimental.pallas import tpu as pltpu
from jax.sharding import PartitionSpec as P

SLOPE = 0.3
BF16 = jnp.bfloat16
F32 = jnp.float32

DEPTH, ROWS, CELLS, C0, C1, C2 = 8, 32, 16, 64, 128, 256
PAIR = 2 * C0
WIDE = CELLS * C0
CHUNKS = 8
DEEP_ROWS = 8 * C1 * C2 // 128 // CHUNKS
EARLY_ROWS = 27 * C0 // CHUNKS
CHUNK_ROWS = DEEP_ROWS + EARLY_ROWS
VMEM_BYTES = 48 * 1024 * 1024


def iota(shape, dim):
    return lax.broadcasted_iota(jnp.int32, shape, dim)


def masked_rows(acts, opens):
    planes = opens.shape[0]
    cells = ROWS * CELLS
    own = (iota((ROWS, cells), 1) // CELLS) == iota((ROWS, cells), 0)
    spread = jnp.concatenate(
        [jnp.where(own, opens[z : z + 1, :], 0).astype(F32).astype(BF16) for z in range(planes)], axis=0
    )
    pick = ((iota((cells, 128), 0) % CELLS) == iota((cells, 128), 1)).astype(F32).astype(BF16)
    by_cell = jnp.dot(spread, pick, preferred_element_type=F32).astype(BF16)
    widen = (iota((128, WIDE), 0) == (iota((128, WIDE), 1) // C0)).astype(F32).astype(BF16)
    mask = jnp.dot(by_cell, widen, preferred_element_type=F32).astype(BF16)
    return acts * mask


def edge_kernel(
    acts_ref, opens_ref, table_ref, w1_hbm, edge_ref, cells_ref, bias_ref, w1_ref, plane_ref, sems
):
    plane = pltpu.make_async_copy(acts_ref.at[DEPTH - 1], plane_ref, sems.at[0])
    cells = pltpu.make_async_copy(opens_ref, cells_ref, sems.at[1])
    table = pltpu.make_async_copy(table_ref, bias_ref, sems.at[2])
    plane.start()
    cells.start()
    table.start()
    early = pltpu.make_async_copy(w1_hbm, w1_ref, sems.at[3])
    early.start()
    cells.wait()
    table.wait()
    plane.wait()
    edge_ref[...] = masked_rows(plane_ref[...], cells_ref[DEPTH - 1 :])
    early.wait()


def places():
    core = lax.axis_index("sample") % 2
    x = (lax.axis_index("sample") // 2) % 2
    y = lax.axis_index("space") % 2
    own = jnp.where(core == 0, 2 * x + y, 2 * y + x)
    other = jnp.where(core == 0, 2 * y + x, 2 * x + y)
    return core, own, other


def chunk_of(m, far):
    core, own, other = places()
    return (1 - core) * 4 + (other ^ m) if far else core * 4 + (own ^ m)


def row_of_slot(q):
    return 2 * (q % 8) + q // 8


def windows(parts):
    return jnp.concatenate(
        [ref[b, top : top + n, x * PAIR : (x + 2) * PAIR] for x in range(CELLS // 2) for ref, b, top, n in parts],
        axis=0,
    )


def tap_weight(w):
    return jnp.concatenate([jnp.zeros((C0, C1), BF16), w], axis=0)


def inner_kernel(
    acts_ref, opens_ref, bias_ref, w1_ref, w2_hbm,
    even_ref, odd_ref, pre_ref, w2_ref,
    sem,
):
    fetch = pltpu.make_async_copy(w2_hbm, w2_ref, sem)
    fetch.start()
    field = masked_rows(acts_ref[...].reshape(DEPTH * ROWS, WIDE), opens_ref[...])
    half = 3 * 64
    r = iota((2 * half, DEPTH * ROWS), 0)
    par = (r >= half).astype(jnp.int32)
    s = r - half * par
    y = 2 * row_of_slot(s % 16) + s // 64 - 1
    z = 2 * ((s % 64) // 16) + par
    want = jnp.where(y >= 0, z * ROWS + y, -1)
    pick = (iota(r.shape, 1) == want).astype(F32).astype(BF16)
    rows = jnp.dot(pick, field, preferred_element_type=F32).astype(BF16)
    for ref, top in ((even_ref, 0), (odd_ref, half)):
        for b in range(3):
            ref[b, :, :PAIR] = jnp.zeros((64, PAIR), BF16)
            ref[b, :, PAIR:] = rows[top + b * 64 : top + (b + 1) * 64]
    pre = bias_ref[...]
    for a, ref in ((1, even_ref), (2, odd_ref)):
        for b in range(3):
            w = tap_weight(w1_ref[a * 3 + b])
            pre = pre + jnp.dot(windows([(ref, b, 0, 64)]), w, preferred_element_type=F32)
    over = jnp.zeros((8 * 48, C1), F32)
    for b in range(3):
        w = tap_weight(w1_ref[b])
        over = over + jnp.dot(windows([(odd_ref, b, 0, 48)]), w, preferred_element_type=F32)
    for x in range(8):
        pre_ref[x * 64 : x * 64 + 16] = pre[x * 64 : x * 64 + 16]
        pre_ref[x * 64 + 16 : (x + 1) * 64] = (
            pre[x * 64 + 16 : (x + 1) * 64] + over[x * 48 : (x + 1) * 48]
        )
    fetch.wait()


def local_kernel(
    below_ref, first_ref, even_ref, odd_ref, pre_ref, w2_ref, cot_ref,
    deep_ref, keep0_ref, keep1_ref, keep2_ref, keep3_ref, send0_ref, send1_ref, send2_ref, send3_ref,
    under_ref, patch_ref, early_ref,
):
    r = iota((48, ROWS), 0)
    y = 2 * row_of_slot(r % 16) + r // 16 - 1
    pick = (iota(r.shape, 1) == y).astype(F32).astype(BF16)
    rows = jnp.dot(pick, below_ref[...], preferred_element_type=F32).astype(BF16)
    for b in range(3):
        under_ref[b, :, :PAIR] = jnp.zeros((16, PAIR), BF16)
        under_ref[b, :, PAIR:] = rows[b * 16 : (b + 1) * 16]
    low = jnp.zeros((8 * 16, C1), F32)
    for b in range(3):
        w = tap_weight(first_ref[b])
        low = low + jnp.dot(windows([(under_ref, b, 0, 16)]), w, preferred_element_type=F32)
    pre = jnp.concatenate(
        [
            part
            for x in range(8)
            for part in (
                pre_ref[x * 64 : x * 64 + 16] + low[x * 16 : (x + 1) * 16],
                pre_ref[x * 64 + 16 : (x + 1) * 64],
            )
        ],
        axis=0,
    )

    def rows_of(a, b):
        if a == 0:
            return windows([(under_ref, b, 0, 16), (odd_ref, b, 0, 48)])
        return windows([(even_ref if a == 1 else odd_ref, b, 0, 64)])

    hidden = jnp.where(pre > 0, pre, SLOPE * pre)

    def piece(xs, zs, a, b, c):
        return (2 * xs + c) * 64 + (2 * zs + a) * 16 + b * 8

    pieces = [(xs, zs) for xs in range(CELLS // 4) for zs in range(DEPTH // 4)]
    taps = [(a, b, c) for a in range(2) for b in range(2) for c in range(2)]
    cot = jnp.concatenate([cot_ref[:, x * C2 : (x + 1) * C2] for x in range(CELLS // 4)], axis=0)
    out = jnp.zeros((64, C2), F32)
    delta_at = {}
    for t, (a, b, c) in enumerate(taps):
        starts = [piece(xs, zs, a, b, c) for xs, zs in pieces]
        patch = jnp.concatenate([hidden[at : at + 8] for at in starts], axis=0).astype(BF16)
        patch_ref[t] = patch
        out = out + jnp.dot(patch, w2_ref[t], preferred_element_type=F32)
        back = lax.dot_general(cot, w2_ref[t], (((1,), (1,)), ((), ())), preferred_element_type=F32)
        for k, at in enumerate(starts):
            delta_at[at] = back[k * 8 : (k + 1) * 8]
    out = out.astype(BF16)
    for x in range(CELLS // 4):
        deep_ref[:, x * C2 : (x + 1) * C2] = out[x * 16 : (x + 1) * 16]
    back = jnp.concatenate([delta_at[at] for at in sorted(delta_at)], axis=0)
    delta = (back * jnp.where(pre > 0, 1.0, SLOPE)).astype(BF16)

    for a in range(3):
        for b in range(3):
            grad = lax.dot_general(
                rows_of(a, b), delta, (((0,), (0,)), ((), ())), preferred_element_type=F32
            )
            at = (a * 3 + b) * 3 * C0
            early_ref[at : at + 3 * C0] = grad[C0:]

    for far in range(2):
        for m in range(4):
            chunk = chunk_of(m, far)
            grad = lax.dot_general(
                patch_ref[chunk], cot, (((0,), (0,)), ((), ())), preferred_element_type=F32
            )
            early = early_ref[pl.ds(pl.multiple_of(chunk * EARLY_ROWS, 8), EARLY_ROWS), :]
            keeps = (keep0_ref, keep1_ref, keep2_ref, keep3_ref)
            ref = ((send0_ref, send1_ref, send2_ref, send3_ref) if far else keeps)[m]
            kind = BF16 if far else F32
            ref[:C1] = grad[:, :128].astype(kind)
            ref[C1 : 2 * C1] = grad[:, 128:].astype(kind)
            ref[2 * C1 :] = early.astype(kind)


def spread_kernel(*refs):
    deep_ref, early_ref, wide_ref, low_ref, sems = refs[8:]
    copies = []
    for k in range(8):
        chunk = chunk_of(k % 4, k // 4)
        wide_ref[k, :, :128] = refs[k][:C1].astype(F32)
        wide_ref[k, :, 128:] = refs[k][C1 : 2 * C1].astype(F32)
        copies.append(pltpu.make_async_copy(wide_ref.at[k], deep_ref.at[chunk], sems.at[2 * k]))
        copies[-1].start()
        low_ref[k] = refs[k][2 * C1 :].astype(F32)
        at = pl.multiple_of(chunk * EARLY_ROWS, 8)
        copies.append(
            pltpu.make_async_copy(
                low_ref.at[k], early_ref.at[pl.ds(at, EARLY_ROWS), :], sems.at[2 * k + 1]
            )
        )
        copies[-1].start()
    for copy in copies:
        copy.wait()


def spread(chunks):
    return pl.pallas_call(
        spread_kernel,
        in_specs=[pl.BlockSpec(memory_space=pltpu.VMEM)] * 8,
        out_specs=[pl.BlockSpec(memory_space=pltpu.HBM)] * 2,
        out_shape=[
            jax.ShapeDtypeStruct((8, C1, C2), F32),
            jax.ShapeDtypeStruct((27 * C0, C1), F32),
        ],
        scratch_shapes=[
            pltpu.VMEM((8, C1, C2), F32),
            pltpu.VMEM((8, EARLY_ROWS, 128), F32),
            pltpu.SemaphoreType.DMA((16,)),
        ],
        compiler_params=pltpu.CompilerParams(vmem_limit_bytes=VMEM_BYTES),
        name="spread_sums",
    )(*chunks)


def swapped(value, flips):
    samples, spaces = lax.axis_size("sample"), lax.axis_size("space")
    pairs = [
        (i * spaces + j, (i ^ flips[i % 2][0]) * spaces + (j ^ flips[i % 2][1]))
        for i in range(samples)
        for j in range(spaces)
    ]
    return lax.ppermute(value, ("sample", "space"), pairs)


SIBLING = ((1, 0), (1, 0))
QUAD = {m: ((m // 2 * 2, m % 2), (m % 2 * 2, m // 2)) for m in (1, 2, 3)}


def total(keep, send):
    got = {m: swapped(send[m], SIBLING) for m in (3, 2, 1, 0)}
    quad = {}
    for m in (3, 2, 1):
        quad[m] = swapped((keep[m] + got[m].astype(F32)).astype(BF16), QUAD[m])
    mine = keep[0] + got[0].astype(F32)
    for m in (3, 2, 1):
        mine = mine + quad[m].astype(F32)
    rest = []
    for axis, bit in (("space", 2), ("sample", 4)):
        while bit < lax.axis_size(axis):
            rest.append((bit, 0) if axis == "sample" else (0, bit))
            bit *= 2
    for flips in zip(rest, rest[::-1]):
        own = mine.astype(BF16)
        mine = own.astype(F32) + swapped(own, flips).astype(F32)
    near = {0: mine.astype(BF16)}
    for m in (3, 2, 1):
        near[m] = swapped(near[0], QUAD[m])
    far = {m: swapped(near[m], SIBLING) for m in range(4)}
    return [near[m] for m in range(4)] + [far[m] for m in range(4)]


def in_hbm(value):
    return pltpu.with_memory_space_constraint(value, pltpu.HBM)


def body(activations, open_cells, wind_class, w_early, bias_table, w_deep, cotangent):
    params = pltpu.CompilerParams(vmem_limit_bytes=VMEM_BYTES)
    acts = activations[0]
    opens = open_cells[0]
    vmem = pl.BlockSpec(memory_space=pltpu.VMEM)
    hbm = pl.BlockSpec(memory_space=pltpu.HBM)
    edge, opens, table, early = pl.pallas_call(
        edge_kernel,
        in_specs=[hbm] * 4,
        out_specs=[vmem] * 4,
        out_shape=[
            jax.ShapeDtypeStruct((ROWS, WIDE), BF16),
            jax.ShapeDtypeStruct(opens.shape, opens.dtype),
            jax.ShapeDtypeStruct(bias_table.shape, bias_table.dtype),
            jax.ShapeDtypeStruct((9, 3 * C0, C1), BF16),
        ],
        scratch_shapes=[pltpu.VMEM((ROWS, WIDE), BF16), pltpu.SemaphoreType.DMA((4,))],
        compiler_params=params,
        name="edge_plane",
    )(in_hbm(acts), in_hbm(opens), in_hbm(bias_table), in_hbm(w_early.reshape(9, 3 * C0, C1)))
    spaces = lax.axis_size("space")
    below = lax.ppermute(edge, "space", [(i, i + 1) for i in range(spaces - 1)])
    chosen = jnp.arange(bias_table.shape[0], dtype=jnp.int32)[:, None] == wind_class[0]
    bias = jnp.sum(jnp.where(chosen, table, jnp.zeros_like(table)), axis=0, keepdims=True)
    pair_rows = jax.ShapeDtypeStruct((3, 64, WIDE + PAIR), BF16)
    inner = pl.pallas_call(
        inner_kernel,
        in_specs=[vmem] * 4 + [hbm],
        out_specs=[vmem] * 4,
        out_shape=[
            pair_rows,
            pair_rows,
            jax.ShapeDtypeStruct((512, C1), F32),
            jax.ShapeDtypeStruct((8, C1, C2), BF16),
        ],
        scratch_shapes=[pltpu.SemaphoreType.DMA],
        compiler_params=params,
        name="inner_terms",
    )(
        acts,
        opens,
        bias,
        early,
        in_hbm(w_deep.reshape(8, C1, C2)),
    )
    deep, *chunks = pl.pallas_call(
        local_kernel,
        in_specs=[vmem] * 7,
        out_specs=[vmem] * 9,
        out_shape=[
            jax.ShapeDtypeStruct((DEPTH // 4 * ROWS // 4, CELLS // 4 * C2), BF16),
        ]
        + [jax.ShapeDtypeStruct((CHUNK_ROWS, 128), F32)] * 4
        + [jax.ShapeDtypeStruct((CHUNK_ROWS, 128), BF16)] * 4,
        scratch_shapes=[
            pltpu.VMEM((3, 16, WIDE + PAIR), BF16),
            pltpu.VMEM((8, 64, C1), BF16),
            pltpu.VMEM((27 * C0, C1), F32),
        ],
        compiler_params=params,
        name="local_terms",
    )(below, early, *inner, cotangent.reshape(DEPTH // 4 * ROWS // 4, CELLS // 4 * C2))
    grad_deep, grad_early = spread(total(chunks[:4], chunks[4:]))
    return (
        deep.reshape(1, DEPTH // 4, ROWS // 4, CELLS // 4 * C2),
        grad_deep.reshape(w_deep.shape),
        grad_early.reshape(w_early.shape),
    )


def solution(mesh):
    in_specs = (
        P("sample", "space", None, None),
        P("sample", "space", None),
        P("sample"),
        P(),
        P(),
        P(),
        P("sample", "space", None, None),
    )
    out_specs = (P("sample", "space", None, None), P(), P())
    return jax.shard_map(body, mesh=mesh, in_specs=in_specs, out_specs=out_specs, check_vma=False)
```

```python
import jax
import jax.numpy as jnp
from jax import lax
from jax.experimental import pallas as pl
from jax.experimental.pallas import tpu as pltpu
from jax.sharding import PartitionSpec as P

SLOPE = 0.3
BF16 = jnp.bfloat16
F32 = jnp.float32

DEPTH, ROWS, CELLS, C0, C1, C2 = 8, 32, 16, 64, 128, 256
PAIR = 2 * C0
WIDE = CELLS * C0
CHUNKS = 8
DEEP_ROWS = 8 * C1 * C2 // 128 // CHUNKS
EARLY_ROWS = 27 * C0 // CHUNKS
CHUNK_ROWS = DEEP_ROWS + EARLY_ROWS
VMEM_BYTES = 48 * 1024 * 1024


def iota(shape, dim):
    return lax.broadcasted_iota(jnp.int32, shape, dim)


def open_rows(opens):
    planes = opens.shape[0]
    cells = ROWS * CELLS
    own = (iota((ROWS, cells), 1) // CELLS) == iota((ROWS, cells), 0)
    spread = jnp.concatenate(
        [jnp.where(own, opens[z : z + 1, :], 0).astype(F32).astype(BF16) for z in range(planes)], axis=0
    )
    pick = ((iota((cells, 128), 0) % CELLS) == iota((cells, 128), 1)).astype(F32).astype(BF16)
    by_cell = jnp.dot(spread, pick, preferred_element_type=F32).astype(BF16)
    widen = (iota((128, WIDE), 0) == (iota((128, WIDE), 1) // C0)).astype(F32).astype(BF16)
    return jnp.dot(by_cell, widen, preferred_element_type=F32).astype(BF16)


def edge_kernel(
    acts_ref, opens_ref, table_ref, w1_hbm, edge_ref, cells_ref, bias_ref, w1_ref, plane_ref, sems
):
    plane = pltpu.make_async_copy(acts_ref.at[DEPTH - 1], plane_ref, sems.at[0])
    cells = pltpu.make_async_copy(opens_ref, cells_ref, sems.at[1])
    table = pltpu.make_async_copy(table_ref, bias_ref, sems.at[2])
    cells.start()
    plane.start()
    table.start()
    early = pltpu.make_async_copy(w1_hbm, w1_ref, sems.at[3])
    early.start()
    cells.wait()
    mask = open_rows(cells_ref[DEPTH - 1 :])
    plane.wait()
    edge_ref[...] = plane_ref[...] * mask
    table.wait()
    early.wait()


def places():
    core = lax.axis_index("sample") % 2
    x = (lax.axis_index("sample") // 2) % 2
    y = lax.axis_index("space") % 2
    own = jnp.where(core == 0, 2 * x + y, 2 * y + x)
    other = jnp.where(core == 0, 2 * y + x, 2 * x + y)
    return core, own, other


def chunk_of(m, far):
    core, own, other = places()
    return (1 - core) * 4 + (other ^ m) if far else core * 4 + (own ^ m)


def row_of_slot(q):
    return 2 * (q % 8) + q // 8


def windows(parts):
    return jnp.concatenate(
        [ref[b, top : top + n, x * PAIR : (x + 2) * PAIR] for x in range(CELLS // 2) for ref, b, top, n in parts],
        axis=0,
    )


def tap_weight(w):
    return jnp.concatenate([jnp.zeros((C0, C1), BF16), w], axis=0)


def inner_kernel(
    acts_ref, opens_ref, bias_ref, w1_ref, w2_hbm,
    even_ref, odd_ref, pre_ref, w2_ref,
    sem,
):
    fetch = pltpu.make_async_copy(w2_hbm, w2_ref, sem)
    fetch.start()
    field = acts_ref[...].reshape(DEPTH * ROWS, WIDE) * open_rows(opens_ref[...])
    half = 3 * 64
    r = iota((2 * half, DEPTH * ROWS), 0)
    par = (r >= half).astype(jnp.int32)
    s = r - half * par
    y = 2 * row_of_slot(s % 16) + s // 64 - 1
    z = 2 * ((s % 64) // 16) + par
    want = jnp.where(y >= 0, z * ROWS + y, -1)
    pick = (iota(r.shape, 1) == want).astype(F32).astype(BF16)
    rows = jnp.dot(pick, field, preferred_element_type=F32).astype(BF16)
    for ref, top in ((even_ref, 0), (odd_ref, half)):
        for b in range(3):
            ref[b, :, :PAIR] = jnp.zeros((64, PAIR), BF16)
            ref[b, :, PAIR:] = rows[top + b * 64 : top + (b + 1) * 64]
    pre = bias_ref[...]
    for a, ref in ((1, even_ref), (2, odd_ref)):
        for b in range(3):
            w = tap_weight(w1_ref[a * 3 + b])
            pre = pre + jnp.dot(windows([(ref, b, 0, 64)]), w, preferred_element_type=F32)
    over = jnp.zeros((8 * 48, C1), F32)
    for b in range(3):
        w = tap_weight(w1_ref[b])
        over = over + jnp.dot(windows([(odd_ref, b, 0, 48)]), w, preferred_element_type=F32)
    for x in range(8):
        pre_ref[x * 64 : x * 64 + 16] = pre[x * 64 : x * 64 + 16]
        pre_ref[x * 64 + 16 : (x + 1) * 64] = (
            pre[x * 64 + 16 : (x + 1) * 64] + over[x * 48 : (x + 1) * 48]
        )
    fetch.wait()


def local_kernel(
    below_ref, first_ref, even_ref, odd_ref, pre_ref, w2_ref, cot_ref,
    deep_ref, keep0_ref, keep1_ref, keep2_ref, keep3_ref, send0_ref, send1_ref, send2_ref, send3_ref,
    under_ref, patch_ref, early_ref,
):
    r = iota((48, ROWS), 0)
    y = 2 * row_of_slot(r % 16) + r // 16 - 1
    pick = (iota(r.shape, 1) == y).astype(F32).astype(BF16)
    rows = jnp.dot(pick, below_ref[...], preferred_element_type=F32).astype(BF16)
    for b in range(3):
        under_ref[b, :, :PAIR] = jnp.zeros((16, PAIR), BF16)
        under_ref[b, :, PAIR:] = rows[b * 16 : (b + 1) * 16]
    low = jnp.zeros((8 * 16, C1), F32)
    for b in range(3):
        w = tap_weight(first_ref[b])
        low = low + jnp.dot(windows([(under_ref, b, 0, 16)]), w, preferred_element_type=F32)
    pre = jnp.concatenate(
        [
            part
            for x in range(8)
            for part in (
                pre_ref[x * 64 : x * 64 + 16] + low[x * 16 : (x + 1) * 16],
                pre_ref[x * 64 + 16 : (x + 1) * 64],
            )
        ],
        axis=0,
    )

    def rows_of(a, b):
        if a == 0:
            return windows([(under_ref, b, 0, 16), (odd_ref, b, 0, 48)])
        return windows([(even_ref if a == 1 else odd_ref, b, 0, 64)])

    hidden = jnp.where(pre > 0, pre, SLOPE * pre)

    def piece(xs, zs, a, b, c):
        return (2 * xs + c) * 64 + (2 * zs + a) * 16 + b * 8

    pieces = [(xs, zs) for xs in range(CELLS // 4) for zs in range(DEPTH // 4)]
    taps = [(a, b, c) for a in range(2) for b in range(2) for c in range(2)]
    cot = jnp.concatenate([cot_ref[:, x * C2 : (x + 1) * C2] for x in range(CELLS // 4)], axis=0)
    out = jnp.zeros((64, C2), F32)
    delta_at = {}
    for t, (a, b, c) in enumerate(taps):
        starts = [piece(xs, zs, a, b, c) for xs, zs in pieces]
        patch = jnp.concatenate([hidden[at : at + 8] for at in starts], axis=0).astype(BF16)
        patch_ref[t] = patch
        out = out + jnp.dot(patch, w2_ref[t], preferred_element_type=F32)
        back = lax.dot_general(cot, w2_ref[t], (((1,), (1,)), ((), ())), preferred_element_type=F32)
        for k, at in enumerate(starts):
            delta_at[at] = back[k * 8 : (k + 1) * 8]
    out = out.astype(BF16)
    for x in range(CELLS // 4):
        deep_ref[:, x * C2 : (x + 1) * C2] = out[x * 16 : (x + 1) * 16]
    back = jnp.concatenate([delta_at[at] for at in sorted(delta_at)], axis=0)
    delta = (back * jnp.where(pre > 0, 1.0, SLOPE)).astype(BF16)

    for a in range(3):
        for b in range(3):
            grad = lax.dot_general(
                delta, rows_of(a, b), (((0,), (0,)), ((), ())), preferred_element_type=F32
            ).T
            at = (a * 3 + b) * 3 * C0
            early_ref[at : at + 3 * C0] = grad[C0:]

    for far in range(2):
        for m in range(4):
            chunk = chunk_of(m, far)
            grad = lax.dot_general(
                patch_ref[chunk], cot, (((0,), (0,)), ((), ())), preferred_element_type=F32
            )
            early = early_ref[pl.ds(pl.multiple_of(chunk * EARLY_ROWS, 8), EARLY_ROWS), :]
            keeps = (keep0_ref, keep1_ref, keep2_ref, keep3_ref)
            ref = ((send0_ref, send1_ref, send2_ref, send3_ref) if far else keeps)[m]
            kind = BF16 if far else F32
            ref[:C1] = grad[:, :128].astype(kind)
            ref[C1 : 2 * C1] = grad[:, 128:].astype(kind)
            ref[2 * C1 :] = early.astype(kind)


def spread_kernel(*refs):
    deep_in, deep_out, wide_out, low_out, wide_ref, low_ref, sems = refs[8:]
    copies = []

    def send(source, target):
        copies.append(pltpu.make_async_copy(source, target, sems.at[len(copies)]))
        copies[-1].start()

    for k in range(8):
        chunk = chunk_of(k % 4, k // 4)
        wide_ref[k, :, :128] = refs[k][:C1].astype(F32)
        wide_ref[k, :, 128:] = refs[k][C1 : 2 * C1].astype(F32)
        send(wide_ref.at[k], wide_out.at[chunk])
        low_ref[k] = refs[k][2 * C1 :].astype(F32)
        at = pl.multiple_of(chunk * EARLY_ROWS, 8)
        send(low_ref.at[k], low_out.at[pl.ds(at, EARLY_ROWS), :])
    send(deep_in, deep_out)
    for copy in copies:
        copy.wait()


def spread(chunks, deep):
    return pl.pallas_call(
        spread_kernel,
        in_specs=[pl.BlockSpec(memory_space=pltpu.VMEM)] * 9,
        out_specs=[pl.BlockSpec(memory_space=pltpu.HBM)] * 3,
        out_shape=[
            jax.ShapeDtypeStruct(deep.shape, BF16),
            jax.ShapeDtypeStruct((8, C1, C2), F32),
            jax.ShapeDtypeStruct((27 * C0, C1), F32),
        ],
        scratch_shapes=[
            pltpu.VMEM((8, C1, C2), F32),
            pltpu.VMEM((8, EARLY_ROWS, 128), F32),
            pltpu.SemaphoreType.DMA((17,)),
        ],
        compiler_params=pltpu.CompilerParams(vmem_limit_bytes=VMEM_BYTES),
        name="spread_sums",
    )(*chunks, deep)


def swapped(value, flips):
    samples, spaces = lax.axis_size("sample"), lax.axis_size("space")
    pairs = [
        (i * spaces + j, (i ^ flips[i % 2][0]) * spaces + (j ^ flips[i % 2][1]))
        for i in range(samples)
        for j in range(spaces)
    ]
    return lax.ppermute(value, ("sample", "space"), pairs)


SIBLING = ((1, 0), (1, 0))
QUAD = {m: ((m // 2 * 2, m % 2), (m % 2 * 2, m // 2)) for m in (1, 2, 3)}


def total(keep, send):
    got = {m: swapped(send[m], SIBLING) for m in (3, 2, 1, 0)}
    quad = {}
    for m in (3, 2, 1):
        quad[m] = swapped((keep[m] + got[m].astype(F32)).astype(BF16), QUAD[m])
    mine = keep[0] + got[0].astype(F32)
    for m in (3, 2, 1):
        mine = mine + quad[m].astype(F32)
    rest = []
    for axis, bit in (("space", 2), ("sample", 4)):
        while bit < lax.axis_size(axis):
            rest.append((bit, 0) if axis == "sample" else (0, bit))
            bit *= 2
    for flips in zip(rest, rest[::-1]):
        own = mine.astype(BF16)
        mine = own.astype(F32) + swapped(own, flips).astype(F32)
    near = {0: mine.astype(BF16)}
    for m in (3, 2, 1):
        near[m] = swapped(near[0], QUAD[m])
    far = {m: swapped(near[m], SIBLING) for m in range(4)}
    return [near[m] for m in range(4)] + [far[m] for m in range(4)]


def in_hbm(value):
    return pltpu.with_memory_space_constraint(value, pltpu.HBM)


def body(activations, open_cells, wind_class, w_early, bias_table, w_deep, cotangent):
    params = pltpu.CompilerParams(vmem_limit_bytes=VMEM_BYTES)
    acts = activations[0]
    opens = open_cells[0]
    vmem = pl.BlockSpec(memory_space=pltpu.VMEM)
    hbm = pl.BlockSpec(memory_space=pltpu.HBM)
    edge, opens, table, early = pl.pallas_call(
        edge_kernel,
        in_specs=[hbm] * 4,
        out_specs=[vmem] * 4,
        out_shape=[
            jax.ShapeDtypeStruct((ROWS, WIDE), BF16),
            jax.ShapeDtypeStruct(opens.shape, opens.dtype),
            jax.ShapeDtypeStruct(bias_table.shape, bias_table.dtype),
            jax.ShapeDtypeStruct((9, 3 * C0, C1), BF16),
        ],
        scratch_shapes=[pltpu.VMEM((ROWS, WIDE), BF16), pltpu.SemaphoreType.DMA((4,))],
        compiler_params=params,
        name="edge_plane",
    )(in_hbm(acts), in_hbm(opens), in_hbm(bias_table), in_hbm(w_early.reshape(9, 3 * C0, C1)))
    spaces = lax.axis_size("space")
    below = lax.ppermute(edge, "space", [(i, i + 1) for i in range(spaces - 1)])
    chosen = jnp.arange(bias_table.shape[0], dtype=jnp.int32)[:, None] == wind_class[0]
    bias = jnp.sum(jnp.where(chosen, table, jnp.zeros_like(table)), axis=0, keepdims=True)
    pair_rows = jax.ShapeDtypeStruct((3, 64, WIDE + PAIR), BF16)
    inner = pl.pallas_call(
        inner_kernel,
        in_specs=[vmem] * 4 + [hbm],
        out_specs=[vmem] * 4,
        out_shape=[
            pair_rows,
            pair_rows,
            jax.ShapeDtypeStruct((512, C1), F32),
            jax.ShapeDtypeStruct((8, C1, C2), BF16),
        ],
        scratch_shapes=[pltpu.SemaphoreType.DMA],
        compiler_params=params,
        name="inner_terms",
    )(
        acts,
        opens,
        bias,
        early,
        in_hbm(w_deep.reshape(8, C1, C2)),
    )
    deep, *chunks = pl.pallas_call(
        local_kernel,
        in_specs=[vmem] * 7,
        out_specs=[vmem] * 9,
        out_shape=[
            jax.ShapeDtypeStruct((DEPTH // 4 * ROWS // 4, CELLS // 4 * C2), BF16),
        ]
        + [jax.ShapeDtypeStruct((CHUNK_ROWS, 128), F32)] * 4
        + [jax.ShapeDtypeStruct((CHUNK_ROWS, 128), BF16)] * 4,
        scratch_shapes=[
            pltpu.VMEM((3, 16, WIDE + PAIR), BF16),
            pltpu.VMEM((8, 64, C1), BF16),
            pltpu.VMEM((27 * C0, C1), F32),
        ],
        compiler_params=params,
        name="local_terms",
    )(below, early, *inner, cotangent.reshape(DEPTH // 4 * ROWS // 4, CELLS // 4 * C2))
    deep, grad_deep, grad_early = spread(total(chunks[:4], chunks[4:]), deep)
    return (
        deep.reshape(1, DEPTH // 4, ROWS // 4, CELLS // 4 * C2),
        grad_deep.reshape(w_deep.shape),
        grad_early.reshape(w_early.shape),
    )


def solution(mesh):
    in_specs = (
        P("sample", "space", None, None),
        P("sample", "space", None),
        P("sample"),
        P(),
        P(),
        P(),
        P("sample", "space", None, None),
    )
    out_specs = (P("sample", "space", None, None), P(), P())
    return jax.shard_map(body, mesh=mesh, in_specs=in_specs, out_specs=out_specs, check_vma=False)
```

```python
import jax
import jax.numpy as jnp
from jax import lax
from jax.experimental import pallas as pl
from jax.experimental.pallas import tpu as pltpu
from jax.sharding import PartitionSpec as P

SLOPE = 0.3
BF16 = jnp.bfloat16
F32 = jnp.float32

DEPTH, ROWS, CELLS, C0, C1, C2 = 8, 32, 16, 64, 128, 256
PAIR = 2 * C0
WIDE = CELLS * C0
CHUNKS = 8
DEEP_ROWS = 8 * C1 * C2 // 128 // CHUNKS
EARLY_ROWS = 27 * C0 // CHUNKS
CHUNK_ROWS = DEEP_ROWS + EARLY_ROWS
VMEM_BYTES = 48 * 1024 * 1024


def iota(shape, dim):
    return lax.broadcasted_iota(jnp.int32, shape, dim)


def open_rows(opens):
    planes = opens.shape[0]
    cells = ROWS * CELLS
    own = (iota((ROWS, cells), 1) // CELLS) == iota((ROWS, cells), 0)
    spread = jnp.concatenate(
        [jnp.where(own, opens[z : z + 1, :], 0).astype(F32).astype(BF16) for z in range(planes)], axis=0
    )
    pick = ((iota((cells, 128), 0) % CELLS) == iota((cells, 128), 1)).astype(F32).astype(BF16)
    by_cell = jnp.dot(spread, pick, preferred_element_type=F32).astype(BF16)
    widen = (iota((128, WIDE), 0) == (iota((128, WIDE), 1) // C0)).astype(F32).astype(BF16)
    return jnp.dot(by_cell, widen, preferred_element_type=F32).astype(BF16)


def edge_kernel(
    acts_ref, opens_ref, table_ref, w1_hbm, cot_hbm,
    edge_ref, cells_ref, bias_ref, w1_ref, cot_ref,
    plane_ref, sems,
):
    plane = pltpu.make_async_copy(acts_ref.at[DEPTH - 1], plane_ref, sems.at[0])
    cells = pltpu.make_async_copy(opens_ref, cells_ref, sems.at[1])
    table = pltpu.make_async_copy(table_ref, bias_ref, sems.at[2])
    cells.start()
    plane.start()
    table.start()
    early = pltpu.make_async_copy(w1_hbm, w1_ref, sems.at[3])
    early.start()
    cot = pltpu.make_async_copy(cot_hbm, cot_ref, sems.at[4])
    cot.start()
    cells.wait()
    mask = open_rows(cells_ref[DEPTH - 1 :])
    plane.wait()
    edge_ref[...] = plane_ref[...] * mask
    table.wait()
    early.wait()
    cot.wait()


def places():
    core = lax.axis_index("sample") % 2
    x = (lax.axis_index("sample") // 2) % 2
    y = lax.axis_index("space") % 2
    own = jnp.where(core == 0, 2 * x + y, 2 * y + x)
    other = jnp.where(core == 0, 2 * y + x, 2 * x + y)
    return core, own, other


def chunk_of(m, far):
    core, own, other = places()
    return (1 - core) * 4 + (other ^ m) if far else core * 4 + (own ^ m)


def row_of_slot(q):
    return 2 * (q % 8) + q // 8


def windows(parts):
    return jnp.concatenate(
        [ref[b, top : top + n, x * PAIR : (x + 2) * PAIR] for x in range(CELLS // 2) for ref, b, top, n in parts],
        axis=0,
    )


def tap_weight(w):
    return jnp.concatenate([jnp.zeros((C0, C1), BF16), w], axis=0)


def blocks(parts):
    return jnp.concatenate(
        [ref[b, top : top + n, (x + 1) * PAIR : (x + 2) * PAIR] for x in range(CELLS // 2) for ref, b, top, n in parts],
        axis=0,
    )


def pair_weight(w):
    here = jnp.concatenate([w[C0 : 2 * C0], jnp.zeros((C0, C1), BF16)], axis=1)
    return jnp.concatenate([here, jnp.concatenate([w[2 * C0 :], w[:C0]], axis=1)], axis=0)


def by_twos(taps):
    return [taps[k : k + 2] for k in range(0, len(taps), 2)]


def convolved(rows, weights, n):
    out = jnp.zeros((rows[0].shape[0], 2 * C1), F32)
    for taps in by_twos(list(zip(rows, weights))):
        left = jnp.concatenate([r for r, _ in taps], axis=1)
        right = jnp.concatenate([pair_weight(w) for _, w in taps], axis=0)
        out = out + jnp.dot(left, right, preferred_element_type=F32)
    ahead = jnp.concatenate([jnp.zeros((n, C1), F32), out[:-n, C1:]], axis=0)
    return out[:, :C1] + ahead


TAPS = [(a, b, c) for a in range(2) for b in range(2) for c in range(2)]


def pieces(tap):
    a, b, c = tap
    return [
        (2 * x + c) * 64 + (2 * z + a) * 16 + b * 8
        for x in range(CELLS // 4)
        for z in range(DEPTH // 4)
    ]


def upstream(cot_ref):
    return jnp.concatenate([cot_ref[:, x * C2 : (x + 1) * C2] for x in range(CELLS // 4)], axis=0)


def inner_kernel(
    acts_ref, opens_ref, bias_ref, w1_ref, cot_ref, w2_hbm,
    even_ref, odd_ref, pre_ref, w2_ref, back_ref,
    sem,
):
    fetch = pltpu.make_async_copy(w2_hbm, w2_ref, sem)
    fetch.start()
    field = acts_ref[...].reshape(DEPTH * ROWS, WIDE) * open_rows(opens_ref[...])
    half = 3 * 64
    r = iota((2 * half, DEPTH * ROWS), 0)
    par = (r >= half).astype(jnp.int32)
    s = r - half * par
    y = 2 * row_of_slot(s % 16) + s // 64 - 1
    z = 2 * ((s % 64) // 16) + par
    want = jnp.where(y >= 0, z * ROWS + y, -1)
    pick = (iota(r.shape, 1) == want).astype(F32).astype(BF16)
    rows = jnp.dot(pick, field, preferred_element_type=F32).astype(BF16)
    for ref, top in ((even_ref, 0), (odd_ref, half)):
        for b in range(3):
            ref[b, :, :PAIR] = jnp.zeros((64, PAIR), BF16)
            ref[b, :, PAIR:] = rows[top + b * 64 : top + (b + 1) * 64]
    pre = bias_ref[...]
    pre = pre + convolved(
        [blocks([(ref, b, 0, 64)]) for ref in (even_ref, odd_ref) for b in range(3)],
        [w1_ref[k] for k in range(3, 9)],
        64,
    )
    over = convolved(
        [blocks([(odd_ref, b, 0, 48)]) for b in range(3)], [w1_ref[b] for b in range(3)], 48
    )
    for x in range(8):
        pre_ref[x * 64 : x * 64 + 16] = pre[x * 64 : x * 64 + 16]
        pre_ref[x * 64 + 16 : (x + 1) * 64] = (
            pre[x * 64 + 16 : (x + 1) * 64] + over[x * 48 : (x + 1) * 48]
        )
    fetch.wait()
    cot = upstream(cot_ref)
    for t, tap in enumerate(TAPS):
        back = lax.dot_general(cot, w2_ref[t], (((1,), (1,)), ((), ())), preferred_element_type=F32)
        for k, at in enumerate(pieces(tap)):
            back_ref[at : at + 8] = back[k * 8 : (k + 1) * 8]


def local_kernel(
    across_ref, beside_ref, first_ref, even_ref, odd_ref, pre_ref, w2_ref, back_ref, cot_ref,
    deep_ref, keep0_ref, keep1_ref, keep2_ref, keep3_ref, send0_ref, send1_ref, send2_ref, send3_ref,
    under_ref, patch_ref, early_ref,
):
    r = iota((48, ROWS), 0)
    y = 2 * row_of_slot(r % 16) + r // 16 - 1
    pick = (iota(r.shape, 1) == y).astype(F32).astype(BF16)
    place = lax.axis_index("space")
    across = jnp.where(place > 0, across_ref[...], 0)
    below = jnp.where(place % 2 == 1, beside_ref[...], across)
    rows = jnp.dot(pick, below, preferred_element_type=F32).astype(BF16)
    for b in range(3):
        under_ref[b, :, :PAIR] = jnp.zeros((16, PAIR), BF16)
        under_ref[b, :, PAIR:] = rows[b * 16 : (b + 1) * 16]
    low = jnp.zeros((8 * 16, C1), F32)
    for b in range(3):
        w = tap_weight(first_ref[b])
        low = low + jnp.dot(windows([(under_ref, b, 0, 16)]), w, preferred_element_type=F32)
    pre = jnp.concatenate(
        [
            part
            for x in range(8)
            for part in (
                pre_ref[x * 64 : x * 64 + 16] + low[x * 16 : (x + 1) * 16],
                pre_ref[x * 64 + 16 : (x + 1) * 64],
            )
        ],
        axis=0,
    )

    def rows_of(a, b):
        if a == 0:
            return windows([(under_ref, b, 0, 16), (odd_ref, b, 0, 48)])
        return windows([(even_ref if a == 1 else odd_ref, b, 0, 64)])

    hidden = jnp.where(pre > 0, pre, SLOPE * pre)

    cot = upstream(cot_ref)
    out = jnp.zeros((64, C2), F32)
    for t, tap in enumerate(TAPS):
        patch = jnp.concatenate([hidden[at : at + 8] for at in pieces(tap)], axis=0).astype(BF16)
        patch_ref[t] = patch
        out = out + jnp.dot(patch, w2_ref[t], preferred_element_type=F32)
    out = out.astype(BF16)
    for x in range(CELLS // 4):
        deep_ref[:, x * C2 : (x + 1) * C2] = out[x * 16 : (x + 1) * 16]
    delta = (back_ref[...] * jnp.where(pre > 0, 1.0, SLOPE)).astype(BF16)

    for a in range(3):
        for b in range(3):
            grad = lax.dot_general(
                delta, rows_of(a, b), (((0,), (0,)), ((), ())), preferred_element_type=F32
            ).T
            at = (a * 3 + b) * 3 * C0
            early_ref[at : at + 3 * C0] = grad[C0:]

    for far in range(2):
        for m in range(4):
            chunk = chunk_of(m, far)
            grad = lax.dot_general(
                patch_ref[chunk], cot, (((0,), (0,)), ((), ())), preferred_element_type=F32
            )
            early = early_ref[pl.ds(pl.multiple_of(chunk * EARLY_ROWS, 8), EARLY_ROWS), :]
            keeps = (keep0_ref, keep1_ref, keep2_ref, keep3_ref)
            ref = ((send0_ref, send1_ref, send2_ref, send3_ref) if far else keeps)[m]
            kind = BF16 if far else F32
            ref[:C1] = grad[:, :128].astype(kind)
            ref[C1 : 2 * C1] = grad[:, 128:].astype(kind)
            ref[2 * C1 :] = early.astype(kind)


def spread_kernel(*refs):
    deep_in, deep_out, wide_out, low_out, wide_ref, low_ref, sems = refs[8:]
    copies = []

    def send(source, target):
        copies.append(pltpu.make_async_copy(source, target, sems.at[len(copies)]))
        copies[-1].start()

    for k in range(8):
        chunk = chunk_of(k % 4, k // 4)
        wide_ref[k, :, :128] = refs[k][:C1].astype(F32)
        wide_ref[k, :, 128:] = refs[k][C1 : 2 * C1].astype(F32)
        send(wide_ref.at[k], wide_out.at[chunk])
        low_ref[k] = refs[k][2 * C1 :].astype(F32)
        at = pl.multiple_of(chunk * EARLY_ROWS, 8)
        send(low_ref.at[k], low_out.at[pl.ds(at, EARLY_ROWS), :])
    send(deep_in, deep_out)
    for copy in copies:
        copy.wait()


def spread(chunks, deep):
    return pl.pallas_call(
        spread_kernel,
        in_specs=[pl.BlockSpec(memory_space=pltpu.VMEM)] * 9,
        out_specs=[pl.BlockSpec(memory_space=pltpu.HBM)] * 3,
        out_shape=[
            jax.ShapeDtypeStruct(deep.shape, BF16),
            jax.ShapeDtypeStruct((8, C1, C2), F32),
            jax.ShapeDtypeStruct((27 * C0, C1), F32),
        ],
        scratch_shapes=[
            pltpu.VMEM((8, C1, C2), F32),
            pltpu.VMEM((8, EARLY_ROWS, 128), F32),
            pltpu.SemaphoreType.DMA((17,)),
        ],
        compiler_params=pltpu.CompilerParams(vmem_limit_bytes=VMEM_BYTES),
        name="spread_sums",
    )(*chunks, deep)


def swapped(value, flips):
    samples, spaces = lax.axis_size("sample"), lax.axis_size("space")
    pairs = [
        (i * spaces + j, (i ^ flips[i % 2][0]) * spaces + (j ^ flips[i % 2][1]))
        for i in range(samples)
        for j in range(spaces)
    ]
    return lax.ppermute(value, ("sample", "space"), pairs)


SIBLING = ((1, 0), (1, 0))
QUAD = {m: ((m // 2 * 2, m % 2), (m % 2 * 2, m // 2)) for m in (1, 2, 3)}


def total(keep, send):
    got = {m: swapped(send[m], SIBLING) for m in (3, 2, 1, 0)}
    quad = {}
    for m in (3, 2, 1):
        quad[m] = swapped((keep[m] + got[m].astype(F32)).astype(BF16), QUAD[m])
    mine = keep[0] + got[0].astype(F32)
    for m in (3, 2, 1):
        mine = mine + quad[m].astype(F32)
    rest = []
    for axis, bit in (("space", 2), ("sample", 4)):
        while bit < lax.axis_size(axis):
            rest.append((bit, 0) if axis == "sample" else (0, bit))
            bit *= 2
    for flips in zip(rest, rest[::-1]):
        own = mine.astype(BF16)
        mine = own.astype(F32) + swapped(own, flips).astype(F32)
    near = {0: mine.astype(BF16)}
    for m in (3, 2, 1):
        near[m] = swapped(near[0], QUAD[m])
    far = {m: swapped(near[m], SIBLING) for m in range(4)}
    return [near[m] for m in range(4)] + [far[m] for m in range(4)]


def neighbours_planes(edge):
    samples, spaces = lax.axis_size("sample"), lax.axis_size("space")

    def partner(i, j):
        k = j - 1 if j % 2 == 0 else j + 1
        return (i, k) if 0 <= k < spaces else (i ^ 1, j)

    places = [(i, j) for i in range(samples) for j in range(spaces)]
    across = [[i * spaces + j for i, j in to] for to in (places, [partner(i, j) for i, j in places])]
    beside = [i * spaces + (j ^ 1) for i, j in places]
    return (
        lax.ppermute(edge, ("sample", "space"), list(zip(*across))),
        lax.ppermute(edge, ("sample", "space"), list(zip(across[0], beside))),
    )


def in_hbm(value):
    return pltpu.with_memory_space_constraint(value, pltpu.HBM)


def body(activations, open_cells, wind_class, w_early, bias_table, w_deep, cotangent):
    params = pltpu.CompilerParams(vmem_limit_bytes=VMEM_BYTES)
    acts = activations[0]
    opens = open_cells[0]
    vmem = pl.BlockSpec(memory_space=pltpu.VMEM)
    hbm = pl.BlockSpec(memory_space=pltpu.HBM)
    flat_cot = cotangent.reshape(DEPTH // 4 * ROWS // 4, CELLS // 4 * C2)
    edge, opens, table, early, cot = pl.pallas_call(
        edge_kernel,
        in_specs=[hbm] * 5,
        out_specs=[vmem] * 5,
        out_shape=[
            jax.ShapeDtypeStruct((ROWS, WIDE), BF16),
            jax.ShapeDtypeStruct(opens.shape, opens.dtype),
            jax.ShapeDtypeStruct(bias_table.shape, bias_table.dtype),
            jax.ShapeDtypeStruct((9, 3 * C0, C1), BF16),
            jax.ShapeDtypeStruct(flat_cot.shape, BF16),
        ],
        scratch_shapes=[pltpu.VMEM((ROWS, WIDE), BF16), pltpu.SemaphoreType.DMA((5,))],
        compiler_params=params,
        name="edge_plane",
    )(
        in_hbm(acts),
        in_hbm(opens),
        in_hbm(bias_table),
        in_hbm(w_early.reshape(9, 3 * C0, C1)),
        in_hbm(flat_cot),
    )
    belows = neighbours_planes(edge)
    chosen = jnp.arange(bias_table.shape[0], dtype=jnp.int32)[:, None] == wind_class[0]
    bias = jnp.sum(jnp.where(chosen, table, jnp.zeros_like(table)), axis=0, keepdims=True)
    pair_rows = jax.ShapeDtypeStruct((3, 64, WIDE + PAIR), BF16)
    inner = pl.pallas_call(
        inner_kernel,
        in_specs=[vmem] * 5 + [hbm],
        out_specs=[vmem] * 5,
        out_shape=[
            pair_rows,
            pair_rows,
            jax.ShapeDtypeStruct((512, C1), F32),
            jax.ShapeDtypeStruct((8, C1, C2), BF16),
            jax.ShapeDtypeStruct((512, C1), F32),
        ],
        scratch_shapes=[pltpu.SemaphoreType.DMA],
        compiler_params=params,
        name="inner_terms",
    )(
        acts,
        opens,
        bias,
        early,
        cot,
        in_hbm(w_deep.reshape(8, C1, C2)),
    )
    deep, *chunks = pl.pallas_call(
        local_kernel,
        in_specs=[vmem] * 9,
        out_specs=[vmem] * 9,
        out_shape=[
            jax.ShapeDtypeStruct((DEPTH // 4 * ROWS // 4, CELLS // 4 * C2), BF16),
        ]
        + [jax.ShapeDtypeStruct((CHUNK_ROWS, 128), F32)] * 4
        + [jax.ShapeDtypeStruct((CHUNK_ROWS, 128), BF16)] * 4,
        scratch_shapes=[
            pltpu.VMEM((3, 16, WIDE + PAIR), BF16),
            pltpu.VMEM((8, 64, C1), BF16),
            pltpu.VMEM((27 * C0, C1), F32),
        ],
        compiler_params=params,
        name="local_terms",
    )(*belows, early, *inner, cot)
    deep, grad_deep, grad_early = spread(total(chunks[:4], chunks[4:]), deep)
    return (
        deep.reshape(1, DEPTH // 4, ROWS // 4, CELLS // 4 * C2),
        grad_deep.reshape(w_deep.shape),
        grad_early.reshape(w_early.shape),
    )


def solution(mesh):
    in_specs = (
        P("sample", "space", None, None),
        P("sample", "space", None),
        P("sample"),
        P(),
        P(),
        P(),
        P("sample", "space", None, None),
    )
    out_specs = (P("sample", "space", None, None), P(), P())
    return jax.shard_map(body, mesh=mesh, in_specs=in_specs, out_specs=out_specs, check_vma=False)
```

```python
import functools

import jax
import jax.numpy as jnp
from jax import lax
from jax.experimental import pallas as pl
from jax.experimental.pallas import tpu as pltpu
from jax.sharding import PartitionSpec as P

SLOPE = 0.3
BF16 = jnp.bfloat16
F32 = jnp.float32

DEPTH, ROWS, CELLS, C0, C1, C2 = 8, 32, 16, 64, 128, 256
PAIR = 2 * C0
WIDE = CELLS * C0
CHUNKS = 8
DEEP_ROWS = 8 * C1 * C2 // 128 // CHUNKS
EARLY_ROWS = 27 * C0 // CHUNKS
CHUNK_ROWS = DEEP_ROWS + EARLY_ROWS
VMEM_BYTES = 48 * 1024 * 1024


def iota(shape, dim):
    return lax.broadcasted_iota(jnp.int32, shape, dim)


def open_rows(opens):
    planes = opens.shape[0]
    cells = ROWS * CELLS
    own = (iota((ROWS, cells), 1) // CELLS) == iota((ROWS, cells), 0)
    spread = jnp.concatenate(
        [jnp.where(own, opens[z : z + 1, :], 0).astype(F32).astype(BF16) for z in range(planes)], axis=0
    )
    pick = ((iota((cells, 128), 0) % CELLS) == iota((cells, 128), 1)).astype(F32).astype(BF16)
    by_cell = jnp.dot(spread, pick, preferred_element_type=F32).astype(BF16)
    widen = (iota((128, WIDE), 0) == (iota((128, WIDE), 1) // C0)).astype(F32).astype(BF16)
    return jnp.dot(by_cell, widen, preferred_element_type=F32).astype(BF16)


def edge_kernel(
    acts_ref, opens_ref, table_ref, w1_hbm, cot_hbm,
    edge_ref, cells_ref, bias_ref, w1_ref, cot_ref,
    plane_ref, sems,
):
    plane = pltpu.make_async_copy(acts_ref.at[DEPTH - 1], plane_ref, sems.at[0])
    cells = pltpu.make_async_copy(opens_ref, cells_ref, sems.at[1])
    table = pltpu.make_async_copy(table_ref, bias_ref, sems.at[2])
    cells.start()
    plane.start()
    table.start()
    early = pltpu.make_async_copy(w1_hbm, w1_ref, sems.at[3])
    early.start()
    cot = pltpu.make_async_copy(cot_hbm, cot_ref, sems.at[4])
    cot.start()
    cells.wait()
    mask = open_rows(cells_ref[DEPTH - 1 :])
    plane.wait()
    edge_ref[...] = plane_ref[...] * mask
    table.wait()
    early.wait()
    cot.wait()


def places():
    core = lax.axis_index("sample") % 2
    x = (lax.axis_index("sample") // 2) % 2
    y = lax.axis_index("space") % 2
    own = jnp.where(core == 0, 2 * x + y, 2 * y + x)
    other = jnp.where(core == 0, 2 * y + x, 2 * x + y)
    return core, own, other


def chunk_of(m, far):
    core, own, other = places()
    return (1 - core) * 4 + (other ^ m) if far else core * 4 + (own ^ m)


def row_of_slot(q):
    return 2 * (q % 8) + q // 8


def windows(parts):
    return jnp.concatenate(
        [ref[b, top : top + n, x * PAIR : (x + 2) * PAIR] for x in range(CELLS // 2) for ref, b, top, n in parts],
        axis=0,
    )


def tap_weight(w):
    return jnp.concatenate([jnp.zeros((C0, C1), BF16), w], axis=0)


def blocks(parts):
    return jnp.concatenate(
        [ref[b, top : top + n, (x + 1) * PAIR : (x + 2) * PAIR] for x in range(CELLS // 2) for ref, b, top, n in parts],
        axis=0,
    )


def pair_weight(w):
    here = jnp.concatenate([w[C0 : 2 * C0], jnp.zeros((C0, C1), BF16)], axis=1)
    return jnp.concatenate([here, jnp.concatenate([w[2 * C0 :], w[:C0]], axis=1)], axis=0)


def by_twos(taps):
    return [taps[k : k + 2] for k in range(0, len(taps), 2)]


def convolved(rows, weights, n):
    out = jnp.zeros((rows[0].shape[0], 2 * C1), F32)
    for taps in by_twos(list(zip(rows, weights))):
        left = jnp.concatenate([r for r, _ in taps], axis=1)
        right = jnp.concatenate([pair_weight(w) for _, w in taps], axis=0)
        out = out + jnp.dot(left, right, preferred_element_type=F32)
    ahead = jnp.concatenate([jnp.zeros((n, C1), F32), out[:-n, C1:]], axis=0)
    return out[:, :C1] + ahead


TAPS = [(a, b, c) for a in range(2) for b in range(2) for c in range(2)]


def pieces(tap):
    a, b, c = tap
    return [
        (2 * x + c) * 64 + (2 * z + a) * 16 + b * 8
        for x in range(CELLS // 4)
        for z in range(DEPTH // 4)
    ]


def upstream(cot_ref):
    return jnp.concatenate([cot_ref[:, x * C2 : (x + 1) * C2] for x in range(CELLS // 4)], axis=0)


def inner_kernel(
    acts_ref, opens_ref, bias_ref, w1_ref, cot_ref, w2_hbm,
    even_ref, odd_ref, pre_ref, w2_ref, back_ref,
    sem,
):
    fetch = pltpu.make_async_copy(w2_hbm, w2_ref, sem)
    fetch.start()
    field = acts_ref[...].reshape(DEPTH * ROWS, WIDE) * open_rows(opens_ref[...])
    half = 3 * 64
    r = iota((2 * half, DEPTH * ROWS), 0)
    par = (r >= half).astype(jnp.int32)
    s = r - half * par
    y = 2 * row_of_slot(s % 16) + s // 64 - 1
    z = 2 * ((s % 64) // 16) + par
    want = jnp.where(y >= 0, z * ROWS + y, -1)
    pick = (iota(r.shape, 1) == want).astype(F32).astype(BF16)
    rows = jnp.dot(pick, field, preferred_element_type=F32).astype(BF16)
    for ref, top in ((even_ref, 0), (odd_ref, half)):
        for b in range(3):
            ref[b, :, :PAIR] = jnp.zeros((64, PAIR), BF16)
            ref[b, :, PAIR:] = rows[top + b * 64 : top + (b + 1) * 64]
    pre = bias_ref[...]
    pre = pre + convolved(
        [blocks([(ref, b, 0, 64)]) for ref in (even_ref, odd_ref) for b in range(3)],
        [w1_ref[k] for k in range(3, 9)],
        64,
    )
    over = convolved(
        [blocks([(odd_ref, b, 0, 48)]) for b in range(3)], [w1_ref[b] for b in range(3)], 48
    )
    for x in range(8):
        pre_ref[x * 64 : x * 64 + 16] = pre[x * 64 : x * 64 + 16]
        pre_ref[x * 64 + 16 : (x + 1) * 64] = (
            pre[x * 64 + 16 : (x + 1) * 64] + over[x * 48 : (x + 1) * 48]
        )
    fetch.wait()
    cot = upstream(cot_ref)
    for t, tap in enumerate(TAPS):
        back = lax.dot_general(cot, w2_ref[t], (((1,), (1,)), ((), ())), preferred_element_type=F32)
        for k, at in enumerate(pieces(tap)):
            back_ref[at : at + 8] = back[k * 8 : (k + 1) * 8]


def local_kernel(
    across_ref, beside_ref, first_ref, even_ref, odd_ref, pre_ref, w2_ref, back_ref, cot_ref,
    deep_ref, keep0_ref, keep1_ref, keep2_ref, keep3_ref, send0_ref, send1_ref, send2_ref, send3_ref,
    under_ref, patch_ref, early_ref,
):
    r = iota((48, ROWS), 0)
    y = 2 * row_of_slot(r % 16) + r // 16 - 1
    pick = (iota(r.shape, 1) == y).astype(F32).astype(BF16)
    place = lax.axis_index("space")
    across = jnp.where(place > 0, across_ref[...], 0)
    below = jnp.where(place % 2 == 1, beside_ref[...], across)
    rows = jnp.dot(pick, below, preferred_element_type=F32).astype(BF16)
    for b in range(3):
        under_ref[b, :, :PAIR] = jnp.zeros((16, PAIR), BF16)
        under_ref[b, :, PAIR:] = rows[b * 16 : (b + 1) * 16]
    low = jnp.zeros((8 * 16, C1), F32)
    for b in range(3):
        w = tap_weight(first_ref[b])
        low = low + jnp.dot(windows([(under_ref, b, 0, 16)]), w, preferred_element_type=F32)
    pre = jnp.concatenate(
        [
            part
            for x in range(8)
            for part in (
                pre_ref[x * 64 : x * 64 + 16] + low[x * 16 : (x + 1) * 16],
                pre_ref[x * 64 + 16 : (x + 1) * 64],
            )
        ],
        axis=0,
    )

    def rows_of(a, b):
        if a == 0:
            return windows([(under_ref, b, 0, 16), (odd_ref, b, 0, 48)])
        return windows([(even_ref if a == 1 else odd_ref, b, 0, 64)])

    hidden = jnp.where(pre > 0, pre, SLOPE * pre)

    cot = upstream(cot_ref)
    out = jnp.zeros((64, C2), F32)
    for t, tap in enumerate(TAPS):
        patch = jnp.concatenate([hidden[at : at + 8] for at in pieces(tap)], axis=0).astype(BF16)
        patch_ref[t] = patch
        out = out + jnp.dot(patch, w2_ref[t], preferred_element_type=F32)
    out = out.astype(BF16)
    for x in range(CELLS // 4):
        deep_ref[:, x * C2 : (x + 1) * C2] = out[x * 16 : (x + 1) * 16]
    delta = (back_ref[...] * jnp.where(pre > 0, 1.0, SLOPE)).astype(BF16)

    for a in range(3):
        for b in range(3):
            grad = lax.dot_general(
                delta, rows_of(a, b), (((0,), (0,)), ((), ())), preferred_element_type=F32
            ).T
            at = (a * 3 + b) * 3 * C0
            early_ref[at : at + 3 * C0] = grad[C0:]

    for far in range(2):
        for m in range(4):
            chunk = chunk_of(m, far)
            grad = lax.dot_general(
                patch_ref[chunk], cot, (((0,), (0,)), ((), ())), preferred_element_type=F32
            )
            early = early_ref[pl.ds(pl.multiple_of(chunk * EARLY_ROWS, 8), EARLY_ROWS), :]
            keeps = (keep0_ref, keep1_ref, keep2_ref, keep3_ref)
            ref = ((send0_ref, send1_ref, send2_ref, send3_ref) if far else keeps)[m]
            kind = BF16 if far else F32
            ref[:C1] = grad[:, :128].astype(kind)
            ref[C1 : 2 * C1] = grad[:, 128:].astype(kind)
            ref[2 * C1 :] = early.astype(kind)


def spread_kernel(names, *refs):
    wide_out, low_out, wide_ref, low_ref, sems = refs[-5:]
    copies = []

    def send(source, target):
        copies.append(pltpu.make_async_copy(source, target, sems.at[len(copies)]))
        copies[-1].start()

    for k, name in enumerate(names):
        chunk = chunk_of(name % 4, name // 4)
        wide_ref[k, :, :128] = refs[k][:C1].astype(F32)
        wide_ref[k, :, 128:] = refs[k][C1 : 2 * C1].astype(F32)
        send(wide_ref.at[k], wide_out.at[chunk])
        low_ref[k] = refs[k][2 * C1 :].astype(F32)
        at = pl.multiple_of(chunk * EARLY_ROWS, 8)
        send(low_ref.at[k], low_out.at[pl.ds(at, EARLY_ROWS), :])
    for copy in copies:
        copy.wait()


def spread(chunks, names, into=()):
    vmem = pl.BlockSpec(memory_space=pltpu.VMEM)
    hbm = pl.BlockSpec(memory_space=pltpu.HBM)
    count = len(names)
    return pl.pallas_call(
        functools.partial(spread_kernel, names),
        in_specs=[vmem] * count + [hbm] * len(into),
        out_specs=[hbm] * 2,
        out_shape=[
            jax.ShapeDtypeStruct((8, C1, C2), F32),
            jax.ShapeDtypeStruct((27 * C0, C1), F32),
        ],
        input_output_aliases={count: 0, count + 1: 1} if into else {},
        scratch_shapes=[
            pltpu.VMEM((count, C1, C2), F32),
            pltpu.VMEM((count, EARLY_ROWS, 128), F32),
            pltpu.SemaphoreType.DMA((2 * count,)),
        ],
        compiler_params=pltpu.CompilerParams(vmem_limit_bytes=VMEM_BYTES),
        name="spread_sums",
    )(*[chunks[k] for k in names], *into)


def swapped(value, flips):
    samples, spaces = lax.axis_size("sample"), lax.axis_size("space")
    pairs = [
        (i * spaces + j, (i ^ flips[i % 2][0]) * spaces + (j ^ flips[i % 2][1]))
        for i in range(samples)
        for j in range(spaces)
    ]
    return lax.ppermute(value, ("sample", "space"), pairs)


SIBLING = ((1, 0), (1, 0))
QUAD = {m: ((m // 2 * 2, m % 2), (m % 2 * 2, m // 2)) for m in (1, 2, 3)}


def total(keep, send):
    got = {m: swapped(send[m], SIBLING) for m in (1, 2, 3, 0)}
    quad = {}
    for m in (1, 2, 3):
        quad[m] = swapped((keep[m] + got[m].astype(F32)).astype(BF16), QUAD[m])
    mine = keep[0] + got[0].astype(F32)
    for m in (1, 2, 3):
        mine = mine + quad[m].astype(F32)
    rest = []
    for axis, bit in (("space", 2), ("sample", 4)):
        while bit < lax.axis_size(axis):
            rest.append((bit, 0) if axis == "sample" else (0, bit))
            bit *= 2
    for flips in zip(rest, rest[::-1]):
        own = mine.astype(BF16)
        mine = own.astype(F32) + swapped(own, flips).astype(F32)
    near = {0: mine.astype(BF16)}
    for m in (3, 1, 2):
        near[m] = swapped(near[0], QUAD[m])
    far = {m: swapped(near[m], SIBLING) for m in range(4)}
    return [near[m] for m in range(4)] + [far[m] for m in range(4)]


def neighbours_planes(edge):
    samples, spaces = lax.axis_size("sample"), lax.axis_size("space")

    def partner(i, j):
        k = j - 1 if j % 2 == 0 else j + 1
        return (i, k) if 0 <= k < spaces else (i ^ 1, j)

    places = [(i, j) for i in range(samples) for j in range(spaces)]
    across = [[i * spaces + j for i, j in to] for to in (places, [partner(i, j) for i, j in places])]
    beside = [i * spaces + (j ^ 1) for i, j in places]
    return (
        lax.ppermute(edge, ("sample", "space"), list(zip(*across))),
        lax.ppermute(edge, ("sample", "space"), list(zip(across[0], beside))),
    )


def in_hbm(value):
    return pltpu.with_memory_space_constraint(value, pltpu.HBM)


def body(activations, open_cells, wind_class, w_early, bias_table, w_deep, cotangent):
    params = pltpu.CompilerParams(vmem_limit_bytes=VMEM_BYTES)
    acts = activations[0]
    opens = open_cells[0]
    vmem = pl.BlockSpec(memory_space=pltpu.VMEM)
    hbm = pl.BlockSpec(memory_space=pltpu.HBM)
    flat_cot = cotangent.reshape(DEPTH // 4 * ROWS // 4, CELLS // 4 * C2)
    edge, opens, table, early, cot = pl.pallas_call(
        edge_kernel,
        in_specs=[hbm] * 5,
        out_specs=[vmem] * 5,
        out_shape=[
            jax.ShapeDtypeStruct((ROWS, WIDE), BF16),
            jax.ShapeDtypeStruct(opens.shape, opens.dtype),
            jax.ShapeDtypeStruct(bias_table.shape, bias_table.dtype),
            jax.ShapeDtypeStruct((9, 3 * C0, C1), BF16),
            jax.ShapeDtypeStruct(flat_cot.shape, BF16),
        ],
        scratch_shapes=[pltpu.VMEM((ROWS, WIDE), BF16), pltpu.SemaphoreType.DMA((5,))],
        compiler_params=params,
        name="edge_plane",
    )(
        in_hbm(acts),
        in_hbm(opens),
        in_hbm(bias_table),
        in_hbm(w_early.reshape(9, 3 * C0, C1)),
        in_hbm(flat_cot),
    )
    belows = neighbours_planes(edge)
    chosen = jnp.arange(bias_table.shape[0], dtype=jnp.int32)[:, None] == wind_class[0]
    bias = jnp.sum(jnp.where(chosen, table, jnp.zeros_like(table)), axis=0, keepdims=True)
    pair_rows = jax.ShapeDtypeStruct((3, 64, WIDE + PAIR), BF16)
    inner = pl.pallas_call(
        inner_kernel,
        in_specs=[vmem] * 5 + [hbm],
        out_specs=[vmem] * 5,
        out_shape=[
            pair_rows,
            pair_rows,
            jax.ShapeDtypeStruct((512, C1), F32),
            jax.ShapeDtypeStruct((8, C1, C2), BF16),
            jax.ShapeDtypeStruct((512, C1), F32),
        ],
        scratch_shapes=[pltpu.SemaphoreType.DMA],
        compiler_params=params,
        name="inner_terms",
    )(
        acts,
        opens,
        bias,
        early,
        cot,
        in_hbm(w_deep.reshape(8, C1, C2)),
    )
    deep, *chunks = pl.pallas_call(
        local_kernel,
        in_specs=[vmem] * 9,
        out_specs=[vmem] * 9,
        out_shape=[
            jax.ShapeDtypeStruct((DEPTH // 4 * ROWS // 4, CELLS // 4 * C2), BF16),
        ]
        + [jax.ShapeDtypeStruct((CHUNK_ROWS, 128), F32)] * 4
        + [jax.ShapeDtypeStruct((CHUNK_ROWS, 128), BF16)] * 4,
        scratch_shapes=[
            pltpu.VMEM((3, 16, WIDE + PAIR), BF16),
            pltpu.VMEM((8, 64, C1), BF16),
            pltpu.VMEM((27 * C0, C1), F32),
        ],
        compiler_params=params,
        name="local_terms",
    )(*belows, early, *inner, cot)
    sums, grads = total(chunks[:4], chunks[4:]), ()
    for names in ((0, 3, 1, 2, 4, 7), (5, 6)):
        grads = spread(sums, names, grads)
    grad_deep, grad_early = grads
    return (
        deep.reshape(1, DEPTH // 4, ROWS // 4, CELLS // 4 * C2),
        grad_deep.reshape(w_deep.shape),
        grad_early.reshape(w_early.shape),
    )


def solution(mesh):
    in_specs = (
        P("sample", "space", None, None),
        P("sample", "space", None),
        P("sample"),
        P(),
        P(),
        P(),
        P("sample", "space", None, None),
    )
    out_specs = (P("sample", "space", None, None), P(), P())
    return jax.shard_map(body, mesh=mesh, in_specs=in_specs, out_specs=out_specs, check_vma=False)
```

```python
import functools

import jax
import jax.numpy as jnp
from jax import lax
from jax.experimental import pallas as pl
from jax.experimental.pallas import tpu as pltpu
from jax.sharding import PartitionSpec as P

SLOPE = 0.3
BF16 = jnp.bfloat16
F32 = jnp.float32

DEPTH, ROWS, CELLS, C0, C1, C2 = 8, 32, 16, 64, 128, 256
PAIR = 2 * C0
WIDE = CELLS * C0
CHUNKS = 8
DEEP_ROWS = 8 * C1 * C2 // 128 // CHUNKS
EARLY_ROWS = 27 * C0 // CHUNKS
CHUNK_ROWS = DEEP_ROWS + EARLY_ROWS
VMEM_BYTES = 48 * 1024 * 1024


def iota(shape, dim):
    return lax.broadcasted_iota(jnp.int32, shape, dim)


def open_rows(opens):
    planes = opens.shape[0]
    cells = ROWS * CELLS
    own = (iota((ROWS, cells), 1) // CELLS) == iota((ROWS, cells), 0)
    spread = jnp.concatenate(
        [jnp.where(own, opens[z : z + 1, :], 0).astype(F32).astype(BF16) for z in range(planes)], axis=0
    )
    pick = ((iota((cells, 128), 0) % CELLS) == iota((cells, 128), 1)).astype(F32).astype(BF16)
    by_cell = jnp.dot(spread, pick, preferred_element_type=F32).astype(BF16)
    widen = (iota((128, WIDE), 0) == (iota((128, WIDE), 1) // C0)).astype(F32).astype(BF16)
    return jnp.dot(by_cell, widen, preferred_element_type=F32).astype(BF16)


def edge_kernel(
    acts_ref, opens_ref, table_ref, w1_hbm, cot_hbm,
    edge_ref, cells_ref, bias_ref, w1_ref, cot_ref,
    plane_ref, sems,
):
    plane = pltpu.make_async_copy(acts_ref.at[DEPTH - 1], plane_ref, sems.at[0])
    cells = pltpu.make_async_copy(opens_ref, cells_ref, sems.at[1])
    table = pltpu.make_async_copy(table_ref, bias_ref, sems.at[2])
    cells.start()
    plane.start()
    table.start()
    early = pltpu.make_async_copy(w1_hbm, w1_ref, sems.at[3])
    early.start()
    cot = pltpu.make_async_copy(cot_hbm, cot_ref, sems.at[4])
    cot.start()
    cells.wait()
    mask = open_rows(cells_ref[DEPTH - 1 :])
    plane.wait()
    edge_ref[...] = plane_ref[...] * mask
    table.wait()
    early.wait()
    cot.wait()


def places():
    core = lax.axis_index("sample") % 2
    x = (lax.axis_index("sample") // 2) % 2
    y = lax.axis_index("space") % 2
    own = jnp.where(core == 0, 2 * x + y, 2 * y + x)
    other = jnp.where(core == 0, 2 * y + x, 2 * x + y)
    return core, own, other


def chunk_of(m, far):
    core, own, other = places()
    return (1 - core) * 4 + (other ^ m) if far else core * 4 + (own ^ m)


def row_of_slot(q):
    return 2 * (q % 8) + q // 8


def windows(parts):
    return jnp.concatenate(
        [ref[b, top : top + n, x * PAIR : (x + 2) * PAIR] for x in range(CELLS // 2) for ref, b, top, n in parts],
        axis=0,
    )


def tap_weight(w):
    return jnp.concatenate([jnp.zeros((C0, C1), BF16), w], axis=0)


def blocks(parts):
    return jnp.concatenate(
        [ref[b, top : top + n, (x + 1) * PAIR : (x + 2) * PAIR] for x in range(CELLS // 2) for ref, b, top, n in parts],
        axis=0,
    )


def pair_weight(w):
    here = jnp.concatenate([w[C0 : 2 * C0], jnp.zeros((C0, C1), BF16)], axis=1)
    return jnp.concatenate([here, jnp.concatenate([w[2 * C0 :], w[:C0]], axis=1)], axis=0)


def by_twos(taps):
    return [taps[k : k + 2] for k in range(0, len(taps), 2)]


def convolved(rows, weights, n):
    out = jnp.zeros((rows[0].shape[0], 2 * C1), F32)
    for taps in by_twos(list(zip(rows, weights))):
        left = jnp.concatenate([r for r, _ in taps], axis=1)
        right = jnp.concatenate([pair_weight(w) for _, w in taps], axis=0)
        out = out + jnp.dot(left, right, preferred_element_type=F32)
    ahead = jnp.concatenate([jnp.zeros((n, C1), F32), out[:-n, C1:]], axis=0)
    return out[:, :C1] + ahead


TAPS = [(a, b, c) for a in range(2) for b in range(2) for c in range(2)]


def pieces(tap):
    a, b, c = tap
    return [
        (2 * x + c) * 64 + (2 * z + a) * 16 + b * 8
        for x in range(CELLS // 4)
        for z in range(DEPTH // 4)
    ]


def upstream(cot_ref):
    return jnp.concatenate([cot_ref[:, x * C2 : (x + 1) * C2] for x in range(CELLS // 4)], axis=0)


def inner_kernel(
    acts_ref, opens_ref, bias_ref, w1_ref, cot_ref, w2_hbm,
    even_ref, odd_ref, pre_ref, w2_ref, back_ref,
    sem,
):
    fetch = pltpu.make_async_copy(w2_hbm, w2_ref, sem)
    fetch.start()
    field = acts_ref[...].reshape(DEPTH * ROWS, WIDE) * open_rows(opens_ref[...])
    half = 3 * 64
    r = iota((2 * half, DEPTH * ROWS), 0)
    par = (r >= half).astype(jnp.int32)
    s = r - half * par
    y = 2 * row_of_slot(s % 16) + s // 64 - 1
    z = 2 * ((s % 64) // 16) + par
    want = jnp.where(y >= 0, z * ROWS + y, -1)
    pick = (iota(r.shape, 1) == want).astype(F32).astype(BF16)
    rows = jnp.dot(pick, field, preferred_element_type=F32).astype(BF16)
    for ref, top in ((even_ref, 0), (odd_ref, half)):
        for b in range(3):
            ref[b, :, :PAIR] = jnp.zeros((64, PAIR), BF16)
            ref[b, :, PAIR:] = rows[top + b * 64 : top + (b + 1) * 64]
    pre = bias_ref[...]
    pre = pre + convolved(
        [blocks([(ref, b, 0, 64)]) for ref in (even_ref, odd_ref) for b in range(3)],
        [w1_ref[k] for k in range(3, 9)],
        64,
    )
    over = convolved(
        [blocks([(odd_ref, b, 0, 48)]) for b in range(3)], [w1_ref[b] for b in range(3)], 48
    )
    for x in range(8):
        pre_ref[x * 64 : x * 64 + 16] = pre[x * 64 : x * 64 + 16]
        pre_ref[x * 64 + 16 : (x + 1) * 64] = (
            pre[x * 64 + 16 : (x + 1) * 64] + over[x * 48 : (x + 1) * 48]
        )
    fetch.wait()
    cot = upstream(cot_ref)
    for t, tap in enumerate(TAPS):
        back = lax.dot_general(cot, w2_ref[t], (((1,), (1,)), ((), ())), preferred_element_type=F32)
        for k, at in enumerate(pieces(tap)):
            back_ref[at : at + 8] = back[k * 8 : (k + 1) * 8]


def local_kernel(
    across_ref, beside_ref, first_ref, even_ref, odd_ref, pre_ref, w2_ref, back_ref, cot_ref,
    deep_ref, keep0_ref, keep1_ref, keep2_ref, keep3_ref, send0_ref, send1_ref, send2_ref, send3_ref,
    under_ref, patch_ref, early_ref,
):
    r = iota((48, ROWS), 0)
    y = 2 * row_of_slot(r % 16) + r // 16 - 1
    pick = (iota(r.shape, 1) == y).astype(F32).astype(BF16)
    place = lax.axis_index("space")
    across = jnp.where(place > 0, across_ref[...], 0)
    below = jnp.where(place % 2 == 1, beside_ref[...], across)
    rows = jnp.dot(pick, below, preferred_element_type=F32).astype(BF16)
    for b in range(3):
        under_ref[b, :, :PAIR] = jnp.zeros((16, PAIR), BF16)
        under_ref[b, :, PAIR:] = rows[b * 16 : (b + 1) * 16]
    low = jnp.zeros((8 * 16, C1), F32)
    for b in range(3):
        w = tap_weight(first_ref[b])
        low = low + jnp.dot(windows([(under_ref, b, 0, 16)]), w, preferred_element_type=F32)
    pre = jnp.concatenate(
        [
            part
            for x in range(8)
            for part in (
                pre_ref[x * 64 : x * 64 + 16] + low[x * 16 : (x + 1) * 16],
                pre_ref[x * 64 + 16 : (x + 1) * 64],
            )
        ],
        axis=0,
    )

    def rows_of(a, b):
        if a == 0:
            return windows([(under_ref, b, 0, 16), (odd_ref, b, 0, 48)])
        return windows([(even_ref if a == 1 else odd_ref, b, 0, 64)])

    hidden = jnp.where(pre > 0, pre, SLOPE * pre)

    cot = upstream(cot_ref)
    out = jnp.zeros((64, C2), F32)
    for t, tap in enumerate(TAPS):
        patch = jnp.concatenate([hidden[at : at + 8] for at in pieces(tap)], axis=0).astype(BF16)
        patch_ref[t] = patch
        out = out + jnp.dot(patch, w2_ref[t], preferred_element_type=F32)
    out = out.astype(BF16)
    for x in range(CELLS // 4):
        deep_ref[:, x * C2 : (x + 1) * C2] = out[x * 16 : (x + 1) * 16]
    delta = (back_ref[...] * jnp.where(pre > 0, 1.0, SLOPE)).astype(BF16)

    for a in range(3):
        for b in range(3):
            grad = lax.dot_general(
                delta, rows_of(a, b), (((0,), (0,)), ((), ())), preferred_element_type=F32
            ).T
            at = (a * 3 + b) * 3 * C0
            early_ref[at : at + 3 * C0] = grad[C0:]

    for far in range(2):
        for m in range(4):
            chunk = chunk_of(m, far)
            grad = lax.dot_general(
                patch_ref[chunk], cot, (((0,), (0,)), ((), ())), preferred_element_type=F32
            )
            early = early_ref[pl.ds(pl.multiple_of(chunk * EARLY_ROWS, 8), EARLY_ROWS), :]
            keeps = (keep0_ref, keep1_ref, keep2_ref, keep3_ref)
            ref = ((send0_ref, send1_ref, send2_ref, send3_ref) if far else keeps)[m]
            kind = BF16 if far else F32
            ref[:C1] = grad[:, :128].astype(kind)
            ref[C1 : 2 * C1] = grad[:, 128:].astype(kind)
            ref[2 * C1 :] = early.astype(kind)


def spread_kernel(names, whole, *refs):
    wide_out, low_out, *whole_out, wide_ref, low_ref, sems = refs[-5 - whole :]
    copies = []

    def send(source, target):
        copies.append(pltpu.make_async_copy(source, target, sems.at[len(copies)]))
        copies[-1].start()

    for k, name in enumerate(names):
        chunk = chunk_of(name % 4, name // 4)
        wide_ref[k, :, :128] = refs[k][:C1].astype(F32)
        wide_ref[k, :, 128:] = refs[k][C1 : 2 * C1].astype(F32)
        send(wide_ref.at[k], wide_out.at[chunk])
        low_ref[k] = refs[k][2 * C1 :].astype(F32)
        at = pl.multiple_of(chunk * EARLY_ROWS, 8)
        send(low_ref.at[k], low_out.at[pl.ds(at, EARLY_ROWS), :])
    for source, target in zip(refs[len(names) :], whole_out):
        send(source, target)
    for copy in copies:
        copy.wait()


def spread(chunks, names, into=(), whole=()):
    vmem = pl.BlockSpec(memory_space=pltpu.VMEM)
    hbm = pl.BlockSpec(memory_space=pltpu.HBM)
    count = len(names)
    return pl.pallas_call(
        functools.partial(spread_kernel, names, len(whole)),
        in_specs=[vmem] * (count + len(whole)) + [hbm] * len(into),
        out_specs=[hbm] * (2 + len(whole)),
        out_shape=[
            jax.ShapeDtypeStruct((8, C1, C2), F32),
            jax.ShapeDtypeStruct((27 * C0, C1), F32),
        ]
        + [jax.ShapeDtypeStruct(value.shape, value.dtype) for value in whole],
        input_output_aliases={count: 0, count + 1: 1} if into else {},
        scratch_shapes=[
            pltpu.VMEM((count, C1, C2), F32),
            pltpu.VMEM((count, EARLY_ROWS, 128), F32),
            pltpu.SemaphoreType.DMA((2 * count + len(whole),)),
        ],
        compiler_params=pltpu.CompilerParams(vmem_limit_bytes=VMEM_BYTES),
        name="spread_sums",
    )(*[chunks[k] for k in names], *whole, *into)


def swapped(value, flips):
    samples, spaces = lax.axis_size("sample"), lax.axis_size("space")
    pairs = [
        (i * spaces + j, (i ^ flips[i % 2][0]) * spaces + (j ^ flips[i % 2][1]))
        for i in range(samples)
        for j in range(spaces)
    ]
    return lax.ppermute(value, ("sample", "space"), pairs)


SIBLING = ((1, 0), (1, 0))
QUAD = {m: ((m // 2 * 2, m % 2), (m % 2 * 2, m // 2)) for m in (1, 2, 3)}


def total(keep, send):
    got = {m: swapped(send[m], SIBLING) for m in (1, 2, 3, 0)}
    quad = {}
    for m in (1, 2, 3):
        quad[m] = swapped((keep[m] + got[m].astype(F32)).astype(BF16), QUAD[m])
    mine = keep[0] + got[0].astype(F32)
    for m in (1, 2, 3):
        mine = mine + quad[m].astype(F32)
    rest = []
    for axis, bit in (("space", 2), ("sample", 4)):
        while bit < lax.axis_size(axis):
            rest.append((bit, 0) if axis == "sample" else (0, bit))
            bit *= 2
    for flips in zip(rest, rest[::-1]):
        own = mine.astype(BF16)
        mine = own.astype(F32) + swapped(own, flips).astype(F32)
    near = {0: mine.astype(BF16)}
    for m in (3, 1, 2):
        near[m] = swapped(near[0], QUAD[m])
    far = {m: swapped(near[m], SIBLING) for m in range(4)}
    return [near[m] for m in range(4)] + [far[m] for m in range(4)]


def neighbours_planes(edge):
    samples, spaces = lax.axis_size("sample"), lax.axis_size("space")

    def partner(i, j):
        k = j - 1 if j % 2 == 0 else j + 1
        return (i, k) if 0 <= k < spaces else (i ^ 1, j)

    places = [(i, j) for i in range(samples) for j in range(spaces)]
    across = [[i * spaces + j for i, j in to] for to in (places, [partner(i, j) for i, j in places])]
    beside = [i * spaces + (j ^ 1) for i, j in places]
    return (
        lax.ppermute(edge, ("sample", "space"), list(zip(*across))),
        lax.ppermute(edge, ("sample", "space"), list(zip(across[0], beside))),
    )


def in_hbm(value):
    return pltpu.with_memory_space_constraint(value, pltpu.HBM)


def body(activations, open_cells, wind_class, w_early, bias_table, w_deep, cotangent):
    params = pltpu.CompilerParams(vmem_limit_bytes=VMEM_BYTES)
    acts = activations[0]
    opens = open_cells[0]
    vmem = pl.BlockSpec(memory_space=pltpu.VMEM)
    hbm = pl.BlockSpec(memory_space=pltpu.HBM)
    flat_cot = cotangent.reshape(DEPTH // 4 * ROWS // 4, CELLS // 4 * C2)
    edge, opens, table, early, cot = pl.pallas_call(
        edge_kernel,
        in_specs=[hbm] * 5,
        out_specs=[vmem] * 5,
        out_shape=[
            jax.ShapeDtypeStruct((ROWS, WIDE), BF16),
            jax.ShapeDtypeStruct(opens.shape, opens.dtype),
            jax.ShapeDtypeStruct(bias_table.shape, bias_table.dtype),
            jax.ShapeDtypeStruct((9, 3 * C0, C1), BF16),
            jax.ShapeDtypeStruct(flat_cot.shape, BF16),
        ],
        scratch_shapes=[pltpu.VMEM((ROWS, WIDE), BF16), pltpu.SemaphoreType.DMA((5,))],
        compiler_params=params,
        name="edge_plane",
    )(
        in_hbm(acts),
        in_hbm(opens),
        in_hbm(bias_table),
        in_hbm(w_early.reshape(9, 3 * C0, C1)),
        in_hbm(flat_cot),
    )
    belows = neighbours_planes(edge)
    chosen = jnp.arange(bias_table.shape[0], dtype=jnp.int32)[:, None] == wind_class[0]
    bias = jnp.sum(jnp.where(chosen, table, jnp.zeros_like(table)), axis=0, keepdims=True)
    pair_rows = jax.ShapeDtypeStruct((3, 64, WIDE + PAIR), BF16)
    inner = pl.pallas_call(
        inner_kernel,
        in_specs=[vmem] * 5 + [hbm],
        out_specs=[vmem] * 5,
        out_shape=[
            pair_rows,
            pair_rows,
            jax.ShapeDtypeStruct((512, C1), F32),
            jax.ShapeDtypeStruct((8, C1, C2), BF16),
            jax.ShapeDtypeStruct((512, C1), F32),
        ],
        scratch_shapes=[pltpu.SemaphoreType.DMA],
        compiler_params=params,
        name="inner_terms",
    )(
        acts,
        opens,
        bias,
        early,
        cot,
        in_hbm(w_deep.reshape(8, C1, C2)),
    )
    deep, *chunks = pl.pallas_call(
        local_kernel,
        in_specs=[vmem] * 9,
        out_specs=[vmem] * 9,
        out_shape=[
            jax.ShapeDtypeStruct((DEPTH // 4 * ROWS // 4, CELLS // 4 * C2), BF16),
        ]
        + [jax.ShapeDtypeStruct((CHUNK_ROWS, 128), F32)] * 4
        + [jax.ShapeDtypeStruct((CHUNK_ROWS, 128), BF16)] * 4,
        scratch_shapes=[
            pltpu.VMEM((3, 16, WIDE + PAIR), BF16),
            pltpu.VMEM((8, 64, C1), BF16),
            pltpu.VMEM((27 * C0, C1), F32),
        ],
        compiler_params=params,
        name="local_terms",
    )(*belows, early, *inner, cot)
    sums = total(chunks[:4], chunks[4:])
    *grads, deep = spread(sums, (0, 3, 1, 2, 4, 7), whole=(deep,))
    grad_deep, grad_early = spread(sums, (5, 6), grads)
    return (
        deep.reshape(1, DEPTH // 4, ROWS // 4, CELLS // 4 * C2),
        grad_deep.reshape(w_deep.shape),
        grad_early.reshape(w_early.shape),
    )


def solution(mesh):
    in_specs = (
        P("sample", "space", None, None),
        P("sample", "space", None),
        P("sample"),
        P(),
        P(),
        P(),
        P("sample", "space", None, None),
    )
    out_specs = (P("sample", "space", None, None), P(), P())
    return jax.shard_map(body, mesh=mesh, in_specs=in_specs, out_specs=out_specs, check_vma=False)
```

```python
import functools

import jax
import jax.numpy as jnp
from jax import lax
from jax.experimental import pallas as pl
from jax.experimental.pallas import tpu as pltpu
from jax.sharding import PartitionSpec as P

SLOPE = 0.3
BF16 = jnp.bfloat16
F32 = jnp.float32

DEPTH, ROWS, CELLS, C0, C1, C2 = 8, 32, 16, 64, 128, 256
PAIR = 2 * C0
WIDE = CELLS * C0
CHUNKS = 8
DEEP_ROWS = 8 * C1 * C2 // 128 // CHUNKS
EARLY_ROWS = 27 * C0 // CHUNKS
CHUNK_ROWS = DEEP_ROWS + EARLY_ROWS
VMEM_BYTES = 48 * 1024 * 1024


def iota(shape, dim):
    return lax.broadcasted_iota(jnp.int32, shape, dim)


def mask_tables():
    cells = ROWS * CELLS
    own = (iota((ROWS, cells), 1) // CELLS) == iota((ROWS, cells), 0)
    pick = ((iota((cells, 128), 0) % CELLS) == iota((cells, 128), 1)).astype(F32).astype(BF16)
    widen = (iota((128, WIDE), 0) == (iota((128, WIDE), 1) // C0)).astype(F32).astype(BF16)
    return own, pick, widen


def open_rows(opens, tables):
    own, pick, widen = tables
    spread = jnp.concatenate(
        [jnp.where(own, opens[z : z + 1, :], 0).astype(F32).astype(BF16) for z in range(opens.shape[0])], axis=0
    )
    by_cell = jnp.dot(spread, pick, preferred_element_type=F32).astype(BF16)
    return jnp.dot(by_cell, widen, preferred_element_type=F32).astype(BF16)


def edge_kernel(
    acts_ref, opens_ref, table_ref, w1_hbm, cot_hbm,
    edge_ref, cells_ref, bias_ref, w1_ref, cot_ref,
    plane_ref, pick_ref, widen_ref, sems,
):
    plane = pltpu.make_async_copy(acts_ref.at[DEPTH - 1], plane_ref, sems.at[0])
    cells = pltpu.make_async_copy(opens_ref, cells_ref, sems.at[1])
    table = pltpu.make_async_copy(table_ref, bias_ref, sems.at[2])
    cells.start()
    plane.start()
    table.start()
    early = pltpu.make_async_copy(w1_hbm, w1_ref, sems.at[3])
    early.start()
    cot = pltpu.make_async_copy(cot_hbm, cot_ref, sems.at[4])
    cot.start()
    pick_ref[...], widen_ref[...] = mask_tables()[1:]
    cells.wait()
    mask = open_rows(cells_ref[DEPTH - 1 :], (mask_tables()[0], pick_ref[...], widen_ref[...]))
    plane.wait()
    edge_ref[...] = plane_ref[...] * mask
    table.wait()
    early.wait()
    cot.wait()


def places():
    core = lax.axis_index("sample") % 2
    x = (lax.axis_index("sample") // 2) % 2
    y = lax.axis_index("space") % 2
    own = jnp.where(core == 0, 2 * x + y, 2 * y + x)
    other = jnp.where(core == 0, 2 * y + x, 2 * x + y)
    return core, own, other


def chunk_of(m, far):
    core, own, other = places()
    return (1 - core) * 4 + (other ^ m) if far else core * 4 + (own ^ m)


def row_of_slot(q):
    return 2 * (q % 8) + q // 8


def windows(parts):
    return jnp.concatenate(
        [ref[b, top : top + n, x * PAIR : (x + 2) * PAIR] for x in range(CELLS // 2) for ref, b, top, n in parts],
        axis=0,
    )


def tap_weight(w):
    return jnp.concatenate([jnp.zeros((C0, C1), BF16), w], axis=0)


def blocks(parts):
    return jnp.concatenate(
        [ref[b, top : top + n, (x + 1) * PAIR : (x + 2) * PAIR] for x in range(CELLS // 2) for ref, b, top, n in parts],
        axis=0,
    )


def pair_weight(w):
    here = jnp.concatenate([w[C0 : 2 * C0], jnp.zeros((C0, C1), BF16)], axis=1)
    return jnp.concatenate([here, jnp.concatenate([w[2 * C0 :], w[:C0]], axis=1)], axis=0)


def by_twos(taps):
    return [taps[k : k + 2] for k in range(0, len(taps), 2)]


def convolved(rows, weights, n):
    out = jnp.zeros((rows[0].shape[0], 2 * C1), F32)
    for taps in by_twos(list(zip(rows, weights))):
        left = jnp.concatenate([r for r, _ in taps], axis=1)
        right = jnp.concatenate([pair_weight(w) for _, w in taps], axis=0)
        out = out + jnp.dot(left, right, preferred_element_type=F32)
    ahead = jnp.concatenate([jnp.zeros((n, C1), F32), out[:-n, C1:]], axis=0)
    return out[:, :C1] + ahead


TAPS = [(a, b, c) for a in range(2) for b in range(2) for c in range(2)]


def pieces(tap):
    a, b, c = tap
    return [
        (2 * x + c) * 64 + (2 * z + a) * 16 + b * 8
        for x in range(CELLS // 4)
        for z in range(DEPTH // 4)
    ]


def upstream(cot_ref):
    return jnp.concatenate([cot_ref[:, x * C2 : (x + 1) * C2] for x in range(CELLS // 4)], axis=0)


def inner_kernel(
    acts_ref, opens_ref, bias_ref, w1_ref, cot_ref, w2_hbm,
    even_ref, odd_ref, pre_ref, w2_ref, back_ref,
    sem,
):
    fetch = pltpu.make_async_copy(w2_hbm, w2_ref, sem)
    fetch.start()
    field = acts_ref[...].reshape(DEPTH * ROWS, WIDE) * open_rows(opens_ref[...], mask_tables())
    half = 3 * 64
    r = iota((2 * half, DEPTH * ROWS), 0)
    par = (r >= half).astype(jnp.int32)
    s = r - half * par
    y = 2 * row_of_slot(s % 16) + s // 64 - 1
    z = 2 * ((s % 64) // 16) + par
    want = jnp.where(y >= 0, z * ROWS + y, -1)
    pick = (iota(r.shape, 1) == want).astype(F32).astype(BF16)
    rows = jnp.dot(pick, field, preferred_element_type=F32).astype(BF16)
    for ref, top in ((even_ref, 0), (odd_ref, half)):
        for b in range(3):
            ref[b, :, :PAIR] = jnp.zeros((64, PAIR), BF16)
            ref[b, :, PAIR:] = rows[top + b * 64 : top + (b + 1) * 64]
    pre = bias_ref[...]
    pre = pre + convolved(
        [blocks([(ref, b, 0, 64)]) for ref in (even_ref, odd_ref) for b in range(3)],
        [w1_ref[k] for k in range(3, 9)],
        64,
    )
    over = convolved(
        [blocks([(odd_ref, b, 0, 48)]) for b in range(3)], [w1_ref[b] for b in range(3)], 48
    )
    for x in range(8):
        pre_ref[x * 64 : x * 64 + 16] = pre[x * 64 : x * 64 + 16]
        pre_ref[x * 64 + 16 : (x + 1) * 64] = (
            pre[x * 64 + 16 : (x + 1) * 64] + over[x * 48 : (x + 1) * 48]
        )
    fetch.wait()
    cot = upstream(cot_ref)
    for t, tap in enumerate(TAPS):
        back = lax.dot_general(cot, w2_ref[t], (((1,), (1,)), ((), ())), preferred_element_type=F32)
        for k, at in enumerate(pieces(tap)):
            back_ref[at : at + 8] = back[k * 8 : (k + 1) * 8]


def local_kernel(
    across_ref, beside_ref, first_ref, even_ref, odd_ref, pre_ref, w2_ref, back_ref, cot_ref,
    deep_ref, keep0_ref, keep1_ref, keep2_ref, keep3_ref, send0_ref, send1_ref, send2_ref, send3_ref,
    under_ref, patch_ref, early_ref,
):
    r = iota((48, ROWS), 0)
    y = 2 * row_of_slot(r % 16) + r // 16 - 1
    pick = (iota(r.shape, 1) == y).astype(F32).astype(BF16)
    place = lax.axis_index("space")
    across = jnp.where(place > 0, across_ref[...], 0)
    below = jnp.where(place % 2 == 1, beside_ref[...], across)
    rows = jnp.dot(pick, below, preferred_element_type=F32).astype(BF16)
    for b in range(3):
        under_ref[b, :, :PAIR] = jnp.zeros((16, PAIR), BF16)
        under_ref[b, :, PAIR:] = rows[b * 16 : (b + 1) * 16]
    low = jnp.zeros((8 * 16, C1), F32)
    for b in range(3):
        w = tap_weight(first_ref[b])
        low = low + jnp.dot(windows([(under_ref, b, 0, 16)]), w, preferred_element_type=F32)
    pre = jnp.concatenate(
        [
            part
            for x in range(8)
            for part in (
                pre_ref[x * 64 : x * 64 + 16] + low[x * 16 : (x + 1) * 16],
                pre_ref[x * 64 + 16 : (x + 1) * 64],
            )
        ],
        axis=0,
    )

    def rows_of(a, b):
        if a == 0:
            return windows([(under_ref, b, 0, 16), (odd_ref, b, 0, 48)])
        return windows([(even_ref if a == 1 else odd_ref, b, 0, 64)])

    hidden = jnp.where(pre > 0, pre, SLOPE * pre)

    cot = upstream(cot_ref)
    out = jnp.zeros((64, C2), F32)
    for t, tap in enumerate(TAPS):
        patch = jnp.concatenate([hidden[at : at + 8] for at in pieces(tap)], axis=0).astype(BF16)
        patch_ref[t] = patch
        out = out + jnp.dot(patch, w2_ref[t], preferred_element_type=F32)
    out = out.astype(BF16)
    for x in range(CELLS // 4):
        deep_ref[:, x * C2 : (x + 1) * C2] = out[x * 16 : (x + 1) * 16]
    delta = (back_ref[...] * jnp.where(pre > 0, 1.0, SLOPE)).astype(BF16)

    for a in range(3):
        for b in range(3):
            grad = lax.dot_general(
                delta, rows_of(a, b), (((0,), (0,)), ((), ())), preferred_element_type=F32
            ).T
            at = (a * 3 + b) * 3 * C0
            early_ref[at : at + 3 * C0] = grad[C0:]

    for far in range(2):
        for m in range(4):
            chunk = chunk_of(m, far)
            grad = lax.dot_general(
                patch_ref[chunk], cot, (((0,), (0,)), ((), ())), preferred_element_type=F32
            )
            early = early_ref[pl.ds(pl.multiple_of(chunk * EARLY_ROWS, 8), EARLY_ROWS), :]
            keeps = (keep0_ref, keep1_ref, keep2_ref, keep3_ref)
            ref = ((send0_ref, send1_ref, send2_ref, send3_ref) if far else keeps)[m]
            kind = BF16 if far else F32
            ref[:C1] = grad[:, :128].astype(kind)
            ref[C1 : 2 * C1] = grad[:, 128:].astype(kind)
            ref[2 * C1 :] = early.astype(kind)


def spread_kernel(names, whole, *refs):
    wide_out, low_out, *whole_out, wide_ref, low_ref, sems = refs[-5 - whole :]
    copies = []

    def send(source, target):
        copies.append(pltpu.make_async_copy(source, target, sems.at[len(copies)]))
        copies[-1].start()

    for k, name in enumerate(names):
        chunk = chunk_of(name % 4, name // 4)
        wide_ref[k, :, :128] = refs[k][:C1].astype(F32)
        wide_ref[k, :, 128:] = refs[k][C1 : 2 * C1].astype(F32)
        send(wide_ref.at[k], wide_out.at[chunk])
        low_ref[k] = refs[k][2 * C1 :].astype(F32)
        at = pl.multiple_of(chunk * EARLY_ROWS, 8)
        send(low_ref.at[k], low_out.at[pl.ds(at, EARLY_ROWS), :])
    for source, target in zip(refs[len(names) :], whole_out):
        send(source, target)
    for copy in copies:
        copy.wait()


def spread(chunks, names, into=(), whole=()):
    vmem = pl.BlockSpec(memory_space=pltpu.VMEM)
    hbm = pl.BlockSpec(memory_space=pltpu.HBM)
    count = len(names)
    return pl.pallas_call(
        functools.partial(spread_kernel, names, len(whole)),
        in_specs=[vmem] * (count + len(whole)) + [hbm] * len(into),
        out_specs=[hbm] * (2 + len(whole)),
        out_shape=[
            jax.ShapeDtypeStruct((8, C1, C2), F32),
            jax.ShapeDtypeStruct((27 * C0, C1), F32),
        ]
        + [jax.ShapeDtypeStruct(value.shape, value.dtype) for value in whole],
        input_output_aliases={count: 0, count + 1: 1} if into else {},
        scratch_shapes=[
            pltpu.VMEM((count, C1, C2), F32),
            pltpu.VMEM((count, EARLY_ROWS, 128), F32),
            pltpu.SemaphoreType.DMA((2 * count + len(whole),)),
        ],
        compiler_params=pltpu.CompilerParams(vmem_limit_bytes=VMEM_BYTES),
        name="spread_sums",
    )(*[chunks[k] for k in names], *whole, *into)


def swapped(value, flips):
    samples, spaces = lax.axis_size("sample"), lax.axis_size("space")
    pairs = [
        (i * spaces + j, (i ^ flips[i % 2][0]) * spaces + (j ^ flips[i % 2][1]))
        for i in range(samples)
        for j in range(spaces)
    ]
    return lax.ppermute(value, ("sample", "space"), pairs)


SIBLING = ((1, 0), (1, 0))
QUAD = {m: ((m // 2 * 2, m % 2), (m % 2 * 2, m // 2)) for m in (1, 2, 3)}


def total(keep, send):
    got = {m: swapped(send[m], SIBLING) for m in (1, 2, 3, 0)}
    quad = {}
    for m in (1, 2, 3):
        quad[m] = swapped((keep[m] + got[m].astype(F32)).astype(BF16), QUAD[m])
    mine = keep[0] + got[0].astype(F32)
    for m in (1, 2, 3):
        mine = mine + quad[m].astype(F32)
    rest = []
    for axis, bit in (("space", 2), ("sample", 4)):
        while bit < lax.axis_size(axis):
            rest.append((bit, 0) if axis == "sample" else (0, bit))
            bit *= 2
    for flips in zip(rest, rest[::-1]):
        own = mine.astype(BF16)
        mine = own.astype(F32) + swapped(own, flips).astype(F32)
    near = {0: mine.astype(BF16)}
    for m in (3, 1, 2):
        near[m] = swapped(near[0], QUAD[m])
    far = {m: swapped(near[m], SIBLING) for m in range(4)}
    return [near[m] for m in range(4)] + [far[m] for m in range(4)]


def neighbours_planes(edge):
    samples, spaces = lax.axis_size("sample"), lax.axis_size("space")

    def partner(i, j):
        k = j - 1 if j % 2 == 0 else j + 1
        return (i, k) if 0 <= k < spaces else (i ^ 1, j)

    places = [(i, j) for i in range(samples) for j in range(spaces)]
    across = [[i * spaces + j for i, j in to] for to in (places, [partner(i, j) for i, j in places])]
    beside = [i * spaces + (j ^ 1) for i, j in places]
    return (
        lax.ppermute(edge, ("sample", "space"), list(zip(*across))),
        lax.ppermute(edge, ("sample", "space"), list(zip(across[0], beside))),
    )


def in_hbm(value):
    return pltpu.with_memory_space_constraint(value, pltpu.HBM)


def body(activations, open_cells, wind_class, w_early, bias_table, w_deep, cotangent):
    params = pltpu.CompilerParams(vmem_limit_bytes=VMEM_BYTES)
    acts = activations[0]
    opens = open_cells[0]
    vmem = pl.BlockSpec(memory_space=pltpu.VMEM)
    hbm = pl.BlockSpec(memory_space=pltpu.HBM)
    flat_cot = cotangent.reshape(DEPTH // 4 * ROWS // 4, CELLS // 4 * C2)
    edge, opens, table, early, cot = pl.pallas_call(
        edge_kernel,
        in_specs=[hbm] * 5,
        out_specs=[vmem] * 5,
        out_shape=[
            jax.ShapeDtypeStruct((ROWS, WIDE), BF16),
            jax.ShapeDtypeStruct(opens.shape, opens.dtype),
            jax.ShapeDtypeStruct(bias_table.shape, bias_table.dtype),
            jax.ShapeDtypeStruct((9, 3 * C0, C1), BF16),
            jax.ShapeDtypeStruct(flat_cot.shape, BF16),
        ],
        scratch_shapes=[
            pltpu.VMEM((ROWS, WIDE), BF16),
            pltpu.VMEM((ROWS * CELLS, 128), BF16),
            pltpu.VMEM((128, WIDE), BF16),
            pltpu.SemaphoreType.DMA((5,)),
        ],
        compiler_params=params,
        name="edge_plane",
    )(
        in_hbm(acts),
        in_hbm(opens),
        in_hbm(bias_table),
        in_hbm(w_early.reshape(9, 3 * C0, C1)),
        in_hbm(flat_cot),
    )
    belows = neighbours_planes(edge)
    chosen = jnp.arange(bias_table.shape[0], dtype=jnp.int32)[:, None] == wind_class[0]
    bias = jnp.sum(jnp.where(chosen, table, jnp.zeros_like(table)), axis=0, keepdims=True)
    pair_rows = jax.ShapeDtypeStruct((3, 64, WIDE + PAIR), BF16)
    inner = pl.pallas_call(
        inner_kernel,
        in_specs=[vmem] * 5 + [hbm],
        out_specs=[vmem] * 5,
        out_shape=[
            pair_rows,
            pair_rows,
            jax.ShapeDtypeStruct((512, C1), F32),
            jax.ShapeDtypeStruct((8, C1, C2), BF16),
            jax.ShapeDtypeStruct((512, C1), F32),
        ],
        scratch_shapes=[pltpu.SemaphoreType.DMA],
        compiler_params=params,
        name="inner_terms",
    )(
        acts,
        opens,
        bias,
        early,
        cot,
        in_hbm(w_deep.reshape(8, C1, C2)),
    )
    deep, *chunks = pl.pallas_call(
        local_kernel,
        in_specs=[vmem] * 9,
        out_specs=[vmem] * 9,
        out_shape=[
            jax.ShapeDtypeStruct((DEPTH // 4 * ROWS // 4, CELLS // 4 * C2), BF16),
        ]
        + [jax.ShapeDtypeStruct((CHUNK_ROWS, 128), F32)] * 4
        + [jax.ShapeDtypeStruct((CHUNK_ROWS, 128), BF16)] * 4,
        scratch_shapes=[
            pltpu.VMEM((3, 16, WIDE + PAIR), BF16),
            pltpu.VMEM((8, 64, C1), BF16),
            pltpu.VMEM((27 * C0, C1), F32),
        ],
        compiler_params=params,
        name="local_terms",
    )(*belows, early, *inner, cot)
    sums = total(chunks[:4], chunks[4:])
    *grads, deep = spread(sums, (0, 3, 1, 2, 4, 7), whole=(deep,))
    grad_deep, grad_early = spread(sums, (5, 6), grads)
    return (
        deep.reshape(1, DEPTH // 4, ROWS // 4, CELLS // 4 * C2),
        grad_deep.reshape(w_deep.shape),
        grad_early.reshape(w_early.shape),
    )


def solution(mesh):
    in_specs = (
        P("sample", "space", None, None),
        P("sample", "space", None),
        P("sample"),
        P(),
        P(),
        P(),
        P("sample", "space", None, None),
    )
    out_specs = (P("sample", "space", None, None), P(), P())
    return jax.shard_map(body, mesh=mesh, in_specs=in_specs, out_specs=out_specs, check_vma=False)
```

```python
import functools

import jax
import jax.numpy as jnp
from jax import lax
from jax.experimental import pallas as pl
from jax.experimental.pallas import tpu as pltpu
from jax.sharding import PartitionSpec as P

SLOPE = 0.3
BF16 = jnp.bfloat16
F32 = jnp.float32

DEPTH, ROWS, CELLS, C0, C1, C2 = 8, 32, 16, 64, 128, 256
PAIR = 2 * C0
WIDE = CELLS * C0
CHUNKS = 8
DEEP_ROWS = 8 * C1 * C2 // 128 // CHUNKS
EARLY_ROWS = 27 * C0 // CHUNKS
CHUNK_ROWS = DEEP_ROWS + EARLY_ROWS
VMEM_BYTES = 48 * 1024 * 1024


def iota(shape, dim):
    return lax.broadcasted_iota(jnp.int32, shape, dim)


def mask_tables():
    cells = ROWS * CELLS
    own = (iota((ROWS, cells), 1) // CELLS) == iota((ROWS, cells), 0)
    pick = ((iota((cells, 128), 0) % CELLS) == iota((cells, 128), 1)).astype(F32).astype(BF16)
    widen = (iota((128, WIDE), 0) == (iota((128, WIDE), 1) // C0)).astype(F32).astype(BF16)
    return own, pick, widen


def open_rows(opens, tables):
    own, pick, widen = tables
    spread = jnp.concatenate(
        [jnp.where(own, opens[z : z + 1, :], 0).astype(F32).astype(BF16) for z in range(opens.shape[0])], axis=0
    )
    by_cell = jnp.dot(spread, pick, preferred_element_type=F32).astype(BF16)
    return jnp.dot(by_cell, widen, preferred_element_type=F32).astype(BF16)


def edge_kernel(
    acts_ref, opens_ref, table_ref, w1_hbm, cot_hbm,
    edge_ref, cells_ref, bias_ref, w1_ref, cot_ref,
    plane_ref, pick_ref, widen_ref, sems,
):
    plane = pltpu.make_async_copy(acts_ref.at[DEPTH - 1], plane_ref, sems.at[0])
    cells = pltpu.make_async_copy(opens_ref, cells_ref, sems.at[1])
    table = pltpu.make_async_copy(table_ref, bias_ref, sems.at[2])
    cells.start()
    plane.start()
    table.start()
    early = pltpu.make_async_copy(w1_hbm, w1_ref, sems.at[3])
    early.start()
    cot = pltpu.make_async_copy(cot_hbm, cot_ref, sems.at[4])
    cot.start()
    pick_ref[...], widen_ref[...] = mask_tables()[1:]
    cells.wait()
    mask = open_rows(cells_ref[DEPTH - 1 :], (mask_tables()[0], pick_ref[...], widen_ref[...]))
    plane.wait()
    edge_ref[...] = plane_ref[...] * mask
    table.wait()
    early.wait()
    cot.wait()


def places():
    core = lax.axis_index("sample") % 2
    x = (lax.axis_index("sample") // 2) % 2
    y = lax.axis_index("space") % 2
    own = jnp.where(core == 0, 2 * x + y, 2 * y + x)
    other = jnp.where(core == 0, 2 * y + x, 2 * x + y)
    return core, own, other


def chunk_of(m, far):
    core, own, other = places()
    return (1 - core) * 4 + (other ^ m) if far else core * 4 + (own ^ m)


def row_of_slot(q):
    return 2 * (q % 8) + q // 8


def windows(parts):
    return jnp.concatenate(
        [ref[b, top : top + n, x * PAIR : (x + 2) * PAIR] for x in range(CELLS // 2) for ref, b, top, n in parts],
        axis=0,
    )


def tap_weight(w):
    return jnp.concatenate([jnp.zeros((C0, C1), BF16), w], axis=0)


def blocks(parts):
    return jnp.concatenate(
        [ref[b, top : top + n, (x + 1) * PAIR : (x + 2) * PAIR] for x in range(CELLS // 2) for ref, b, top, n in parts],
        axis=0,
    )


def pair_weight(w):
    here = jnp.concatenate([w[C0 : 2 * C0], jnp.zeros((C0, C1), BF16)], axis=1)
    return jnp.concatenate([here, jnp.concatenate([w[2 * C0 :], w[:C0]], axis=1)], axis=0)


def by_twos(taps):
    return [taps[k : k + 2] for k in range(0, len(taps), 2)]


def convolved(rows, weights, n):
    out = jnp.zeros((rows[0].shape[0], 2 * C1), F32)
    for taps in by_twos(list(zip(rows, weights))):
        left = jnp.concatenate([r for r, _ in taps], axis=1)
        right = jnp.concatenate([pair_weight(w) for _, w in taps], axis=0)
        out = out + jnp.dot(left, right, preferred_element_type=F32)
    ahead = jnp.concatenate([jnp.zeros((n, C1), F32), out[:-n, C1:]], axis=0)
    return out[:, :C1] + ahead


TAPS = [(a, b, c) for a in range(2) for b in range(2) for c in range(2)]


def pieces(tap):
    a, b, c = tap
    return [
        (2 * x + c) * 64 + (2 * z + a) * 16 + b * 8
        for x in range(CELLS // 4)
        for z in range(DEPTH // 4)
    ]


def upstream(cot_ref):
    return jnp.concatenate([cot_ref[:, x * C2 : (x + 1) * C2] for x in range(CELLS // 4)], axis=0)


def inner_kernel(
    acts_ref, opens_ref, bias_ref, w1_ref, cot_ref, w2_hbm,
    even_ref, odd_ref, pre_ref, w2_ref, back_ref,
    sem,
):
    fetch = pltpu.make_async_copy(w2_hbm, w2_ref, sem)
    fetch.start()
    field = acts_ref[...].reshape(DEPTH * ROWS, WIDE) * open_rows(opens_ref[...], mask_tables())
    half = 3 * 64
    r = iota((2 * half, DEPTH * ROWS), 0)
    par = (r >= half).astype(jnp.int32)
    s = r - half * par
    y = 2 * row_of_slot(s % 16) + s // 64 - 1
    z = 2 * ((s % 64) // 16) + par
    want = jnp.where(y >= 0, z * ROWS + y, -1)
    pick = (iota(r.shape, 1) == want).astype(F32).astype(BF16)
    rows = jnp.dot(pick, field, preferred_element_type=F32).astype(BF16)
    for ref, top in ((even_ref, 0), (odd_ref, half)):
        for b in range(3):
            ref[b, :, :PAIR] = jnp.zeros((64, PAIR), BF16)
            ref[b, :, PAIR:] = rows[top + b * 64 : top + (b + 1) * 64]
    pre = bias_ref[...]
    pre = pre + convolved(
        [blocks([(ref, b, 0, 64)]) for ref in (even_ref, odd_ref) for b in range(3)],
        [w1_ref[k] for k in range(3, 9)],
        64,
    )
    over = convolved(
        [blocks([(odd_ref, b, 0, 48)]) for b in range(3)], [w1_ref[b] for b in range(3)], 48
    )
    for x in range(8):
        pre_ref[x * 64 : x * 64 + 16] = pre[x * 64 : x * 64 + 16]
        pre_ref[x * 64 + 16 : (x + 1) * 64] = (
            pre[x * 64 + 16 : (x + 1) * 64] + over[x * 48 : (x + 1) * 48]
        )
    fetch.wait()
    cot = upstream(cot_ref)
    for t, tap in enumerate(TAPS):
        back = lax.dot_general(cot, w2_ref[t], (((1,), (1,)), ((), ())), preferred_element_type=F32)
        for k, at in enumerate(pieces(tap)):
            back_ref[at : at + 8] = back[k * 8 : (k + 1) * 8]


def local_kernel(
    across_ref, beside_ref, first_ref, even_ref, odd_ref, pre_ref, w2_ref, back_ref, cot_ref,
    deep_ref, keep0_ref, keep1_ref, keep2_ref, keep3_ref, send0_ref, send1_ref, send2_ref, send3_ref,
    under_ref, patch_ref, early_ref,
):
    r = iota((48, ROWS), 0)
    y = 2 * row_of_slot(r % 16) + r // 16 - 1
    pick = (iota(r.shape, 1) == y).astype(F32).astype(BF16)
    place = lax.axis_index("space")
    across = jnp.where(place > 0, across_ref[...], 0)
    below = jnp.where(place % 2 == 1, beside_ref[...], across)
    rows = jnp.dot(pick, below, preferred_element_type=F32).astype(BF16)
    for b in range(3):
        under_ref[b, :, :PAIR] = jnp.zeros((16, PAIR), BF16)
        under_ref[b, :, PAIR:] = rows[b * 16 : (b + 1) * 16]
    low = jnp.zeros((8 * 16, C1), F32)
    for b in range(3):
        w = tap_weight(first_ref[b])
        low = low + jnp.dot(windows([(under_ref, b, 0, 16)]), w, preferred_element_type=F32)
    pre = jnp.concatenate(
        [
            part
            for x in range(8)
            for part in (
                pre_ref[x * 64 : x * 64 + 16] + low[x * 16 : (x + 1) * 16],
                pre_ref[x * 64 + 16 : (x + 1) * 64],
            )
        ],
        axis=0,
    )

    def rows_of(a, b):
        if a == 0:
            return windows([(under_ref, b, 0, 16), (odd_ref, b, 0, 48)])
        return windows([(even_ref if a == 1 else odd_ref, b, 0, 64)])

    hidden = jnp.where(pre > 0, pre, SLOPE * pre)

    cot = upstream(cot_ref)
    out = jnp.zeros((64, C2), F32)
    for t, tap in enumerate(TAPS):
        patch = jnp.concatenate([hidden[at : at + 8] for at in pieces(tap)], axis=0).astype(BF16)
        patch_ref[t] = patch
        out = out + jnp.dot(patch, w2_ref[t], preferred_element_type=F32)
    out = out.astype(BF16)
    for x in range(CELLS // 4):
        deep_ref[:, x * C2 : (x + 1) * C2] = out[x * 16 : (x + 1) * 16]
    delta = (back_ref[...] * jnp.where(pre > 0, 1.0, SLOPE)).astype(BF16)

    for a in range(3):
        for b in range(3):
            grad = lax.dot_general(
                delta, rows_of(a, b), (((0,), (0,)), ((), ())), preferred_element_type=F32
            ).T
            at = (a * 3 + b) * 3 * C0
            early_ref[at : at + 3 * C0] = grad[C0:]

    for far in range(2):
        for m in range(4):
            chunk = chunk_of(m, far)
            grad = lax.dot_general(
                patch_ref[chunk], cot, (((0,), (0,)), ((), ())), preferred_element_type=F32
            )
            early = early_ref[pl.ds(pl.multiple_of(chunk * EARLY_ROWS, 8), EARLY_ROWS), :]
            keeps = (keep0_ref, keep1_ref, keep2_ref, keep3_ref)
            ref = ((send0_ref, send1_ref, send2_ref, send3_ref) if far else keeps)[m]
            kind = BF16 if far else F32
            ref[:C1] = grad[:, :128].astype(kind)
            ref[C1 : 2 * C1] = grad[:, 128:].astype(kind)
            ref[2 * C1 :] = early.astype(kind)


def spread_kernel(names, whole, *refs):
    wide_out, low_out, *whole_out, wide_ref, low_ref, sems = refs[-5 - whole :]
    copies = []

    def send(source, target):
        copies.append(pltpu.make_async_copy(source, target, sems.at[len(copies)]))
        copies[-1].start()

    for k, name in enumerate(names):
        chunk = chunk_of(name % 4, name // 4)
        wide_ref[k, :, :128] = refs[k][:C1].astype(F32)
        wide_ref[k, :, 128:] = refs[k][C1 : 2 * C1].astype(F32)
        send(wide_ref.at[k], wide_out.at[chunk])
        low_ref[k] = refs[k][2 * C1 :].astype(F32)
        at = pl.multiple_of(chunk * EARLY_ROWS, 8)
        send(low_ref.at[k], low_out.at[pl.ds(at, EARLY_ROWS), :])
    for source, target in zip(refs[len(names) :], whole_out):
        send(source, target)
    for copy in copies:
        copy.wait()


def spread(chunks, names, into=(), whole=()):
    vmem = pl.BlockSpec(memory_space=pltpu.VMEM)
    hbm = pl.BlockSpec(memory_space=pltpu.HBM)
    count = len(names)
    return pl.pallas_call(
        functools.partial(spread_kernel, names, len(whole)),
        in_specs=[vmem] * (count + len(whole)) + [hbm] * len(into),
        out_specs=[hbm] * (2 + len(whole)),
        out_shape=[
            jax.ShapeDtypeStruct((8, C1, C2), F32),
            jax.ShapeDtypeStruct((27 * C0, C1), F32),
        ]
        + [jax.ShapeDtypeStruct(value.shape, value.dtype) for value in whole],
        input_output_aliases={count: 0, count + 1: 1} if into else {},
        scratch_shapes=[
            pltpu.VMEM((count, C1, C2), F32),
            pltpu.VMEM((count, EARLY_ROWS, 128), F32),
            pltpu.SemaphoreType.DMA((2 * count + len(whole),)),
        ],
        compiler_params=pltpu.CompilerParams(vmem_limit_bytes=VMEM_BYTES),
        name="spread_sums",
    )(*[chunks[k] for k in names], *whole, *into)


def swapped(value, flips):
    samples, spaces = lax.axis_size("sample"), lax.axis_size("space")
    pairs = [
        (i * spaces + j, (i ^ flips[i % 2][0]) * spaces + (j ^ flips[i % 2][1]))
        for i in range(samples)
        for j in range(spaces)
    ]
    return lax.ppermute(value, ("sample", "space"), pairs)


SIBLING = ((1, 0), (1, 0))
QUAD = {m: ((m // 2 * 2, m % 2), (m % 2 * 2, m // 2)) for m in (1, 2, 3)}


def total(keep, send):
    got = {m: swapped(send[m], SIBLING) for m in (1, 2, 0, 3)}
    quad = {}
    for m in (1, 2, 3):
        quad[m] = swapped((keep[m] + got[m].astype(F32)).astype(BF16), QUAD[m])
    mine = keep[0] + got[0].astype(F32)
    for m in (1, 2, 3):
        mine = mine + quad[m].astype(F32)
    rest = []
    for axis, bit in (("space", 2), ("sample", 4)):
        while bit < lax.axis_size(axis):
            rest.append((bit, 0) if axis == "sample" else (0, bit))
            bit *= 2
    for flips in zip(rest, rest[::-1]):
        own = mine.astype(BF16)
        mine = own.astype(F32) + swapped(own, flips).astype(F32)
    near = {0: mine.astype(BF16)}
    for m in (3, 1, 2):
        near[m] = swapped(near[0], QUAD[m])
    far = {m: swapped(near[m], SIBLING) for m in range(4)}
    return [near[m] for m in range(4)] + [far[m] for m in range(4)]


def neighbours_planes(edge):
    samples, spaces = lax.axis_size("sample"), lax.axis_size("space")

    def partner(i, j):
        k = j - 1 if j % 2 == 0 else j + 1
        return (i, k) if 0 <= k < spaces else (i ^ 1, j)

    places = [(i, j) for i in range(samples) for j in range(spaces)]
    across = [[i * spaces + j for i, j in to] for to in (places, [partner(i, j) for i, j in places])]
    beside = [i * spaces + (j ^ 1) for i, j in places]
    return (
        lax.ppermute(edge, ("sample", "space"), list(zip(*across))),
        lax.ppermute(edge, ("sample", "space"), list(zip(across[0], beside))),
    )


def in_hbm(value):
    return pltpu.with_memory_space_constraint(value, pltpu.HBM)


def body(activations, open_cells, wind_class, w_early, bias_table, w_deep, cotangent):
    params = pltpu.CompilerParams(vmem_limit_bytes=VMEM_BYTES)
    acts = activations[0]
    opens = open_cells[0]
    vmem = pl.BlockSpec(memory_space=pltpu.VMEM)
    hbm = pl.BlockSpec(memory_space=pltpu.HBM)
    flat_cot = cotangent.reshape(DEPTH // 4 * ROWS // 4, CELLS // 4 * C2)
    edge, opens, table, early, cot = pl.pallas_call(
        edge_kernel,
        in_specs=[hbm] * 5,
        out_specs=[vmem] * 5,
        out_shape=[
            jax.ShapeDtypeStruct((ROWS, WIDE), BF16),
            jax.ShapeDtypeStruct(opens.shape, opens.dtype),
            jax.ShapeDtypeStruct(bias_table.shape, bias_table.dtype),
            jax.ShapeDtypeStruct((9, 3 * C0, C1), BF16),
            jax.ShapeDtypeStruct(flat_cot.shape, BF16),
        ],
        scratch_shapes=[
            pltpu.VMEM((ROWS, WIDE), BF16),
            pltpu.VMEM((ROWS * CELLS, 128), BF16),
            pltpu.VMEM((128, WIDE), BF16),
            pltpu.SemaphoreType.DMA((5,)),
        ],
        compiler_params=params,
        name="edge_plane",
    )(
        in_hbm(acts),
        in_hbm(opens),
        in_hbm(bias_table),
        in_hbm(w_early.reshape(9, 3 * C0, C1)),
        in_hbm(flat_cot),
    )
    belows = neighbours_planes(edge)
    chosen = jnp.arange(bias_table.shape[0], dtype=jnp.int32)[:, None] == wind_class[0]
    bias = jnp.sum(jnp.where(chosen, table, jnp.zeros_like(table)), axis=0, keepdims=True)
    pair_rows = jax.ShapeDtypeStruct((3, 64, WIDE + PAIR), BF16)
    inner = pl.pallas_call(
        inner_kernel,
        in_specs=[vmem] * 5 + [hbm],
        out_specs=[vmem] * 5,
        out_shape=[
            pair_rows,
            pair_rows,
            jax.ShapeDtypeStruct((512, C1), F32),
            jax.ShapeDtypeStruct((8, C1, C2), BF16),
            jax.ShapeDtypeStruct((512, C1), F32),
        ],
        scratch_shapes=[pltpu.SemaphoreType.DMA],
        compiler_params=params,
        name="inner_terms",
    )(
        acts,
        opens,
        bias,
        early,
        cot,
        in_hbm(w_deep.reshape(8, C1, C2)),
    )
    deep, *chunks = pl.pallas_call(
        local_kernel,
        in_specs=[vmem] * 9,
        out_specs=[vmem] * 9,
        out_shape=[
            jax.ShapeDtypeStruct((DEPTH // 4 * ROWS // 4, CELLS // 4 * C2), BF16),
        ]
        + [jax.ShapeDtypeStruct((CHUNK_ROWS, 128), F32)] * 4
        + [jax.ShapeDtypeStruct((CHUNK_ROWS, 128), BF16)] * 4,
        scratch_shapes=[
            pltpu.VMEM((3, 16, WIDE + PAIR), BF16),
            pltpu.VMEM((8, 64, C1), BF16),
            pltpu.VMEM((27 * C0, C1), F32),
        ],
        compiler_params=params,
        name="local_terms",
    )(*belows, early, *inner, cot)
    sums = total(chunks[:4], chunks[4:])
    *grads, deep = spread(sums, (0, 3, 1, 2, 4, 7), whole=(deep,))
    grad_deep, grad_early = spread(sums, (5, 6), grads)
    return (
        deep.reshape(1, DEPTH // 4, ROWS // 4, CELLS // 4 * C2),
        grad_deep.reshape(w_deep.shape),
        grad_early.reshape(w_early.shape),
    )


def solution(mesh):
    in_specs = (
        P("sample", "space", None, None),
        P("sample", "space", None),
        P("sample"),
        P(),
        P(),
        P(),
        P("sample", "space", None, None),
    )
    out_specs = (P("sample", "space", None, None), P(), P())
    return jax.shard_map(body, mesh=mesh, in_specs=in_specs, out_specs=out_specs, check_vma=False)
```
